32 devices in a mesh: dp: 4 (over y, core), seq: 8 (over z, x).
Axes of the slice: x: 2, y: 2, z: 4, core: 2. Of those that a mesh axis runs over, the one named last changes fastest.
Arguments:
- tokens: bfloat16 [4, 1024, 2048], P('dp', 'seq'), may hold values from -6 to 6
- query_proj: bfloat16 [2048, 1024], P(('dp', 'seq')), may hold values from -0.125 to 0.125
- key_proj: bfloat16 [2048, 1024], P(('dp', 'seq')), may hold values from -0.125 to 0.125
- value_proj: bfloat16 [2048, 2048], P(('dp', 'seq')), may hold values from -0.125 to 0.125
- swish_proj: bfloat16 [2048, 2048], P(('dp', 'seq')), may hold values from -0.125 to 0.125
- rank_in: bfloat16 [2048, 16], P(('dp', 'seq')), may hold values from -0.125 to 0.125
- rank_out: bfloat16 [1024, 16], P(('dp', 'seq')), may hold values from -1.5 to 1.5
- decay_bias: bfloat16 [1024], P(('dp', 'seq')), may hold values from 0.5 to 10
- attn_gain: bfloat16 [2048], P(('dp', 'seq')), may hold values from 0.5 to 1.5
- head_gain: bfloat16 [512], P(('dp', 'seq')), may hold values from 0.5 to 1.5
- out_proj: bfloat16 [2048, 2048], P(('dp', 'seq')), may hold values from -0.1875 to 0.1875
- mlp_gain: bfloat16 [2048], P(('dp', 'seq')), may hold values from 0.5 to 1.5
- gate_proj: bfloat16 [2048, 5632], P(('dp', 'seq')), may hold values from -0.125 to 0.125
- up_proj: bfloat16 [2048, 5632], P(('dp', 'seq')), may hold values from -0.125 to 0.125
- down_proj: bfloat16 [5632, 2048], P(('dp', 'seq')), may hold values from -0.078125 to 0.078125
- cotangent: bfloat16 [4, 1024, 2048], P('dp', 'seq'), may hold values from -6 to 6
Outputs:
- block_out: bfloat16 [4, 1024, 2048], P('dp', 'seq')
- grad_tokens: bfloat16 [4, 1024, 2048], P('dp', 'seq')
- grad_query: float32 [2048, 1024], P(('dp', 'seq'))
- grad_key: float32 [2048, 1024], P(('dp', 'seq'))
- grad_value: float32 [2048, 2048], P(('dp', 'seq'))
- grad_swish: float32 [2048, 2048], P(('dp', 'seq'))
- grad_rankin: float32 [2048, 16], P(('dp', 'seq'))
- grad_rankout: float32 [1024, 16], P(('dp', 'seq'))
- grad_bias: float32 [1024], P(('dp', 'seq'))
- grad_attngain: float32 [2048], P(('dp', 'seq'))
- grad_headgain: float32 [512], P(('dp', 'seq'))
- grad_outproj: float32 [2048, 2048], P(('dp', 'seq'))
- grad_mlpgain: float32 [2048], P(('dp', 'seq'))
- grad_gate: float32 [2048, 5632], P(('dp', 'seq'))
- grad_upproj: float32 [2048, 5632], P(('dp', 'seq'))
- grad_down: float32 [5632, 2048], P(('dp', 'seq'))
The draws below stay inside these ranges and needn't reach their ends.
All inputs are finite; a program needn't handle non-finite values.
Results may differ from the reference program's by a relative error of at most 0.025.
Values may be sent and summed in bfloat16 or wider, within the bound.
No kernel may reach another device: no remote copies, remote signals or barrier semaphores. Data moves between devices by JAX's collectives and lax.ppermute only.
A program may use at most 640 MiB of HBM per device.

```python
import jax
import jax.numpy as jnp
from jax import lax

D = 2048
HEADS = 4
HD = 512
KD = 1024
RANK = 16
FF = 5632
BLOCK = 64
SEQS = 4
LEN = 1024


def shard_levels(key, shape, shards, smallest, high):
    level = 1.0
    for position, blocks in shards:
        draws = jax.random.uniform(jax.random.fold_in(jax.random.fold_in(key, 6), position), (blocks,), jnp.float32, smallest / len(shards), high / len(shards))
        level = level * jnp.repeat(jnp.exp(draws), shape[position] // blocks).reshape((-1,) + (1,) * (len(shape) - 1 - position))
    return level


def centred(own_key, shape, width, reach, pieces=(), kind=jnp.bfloat16):
    values = width * jax.random.normal(own_key, shape, jnp.float32)
    if pieces:
        values = values * shard_levels(own_key, shape, pieces, -0.22, 0.18)
    return jnp.clip(values, -reach, reach).astype(kind)


def setup_inputs(seed: int = 0) -> dict:
    splits = jax.random.split(jax.random.key(seed), 17)
    tokens = centred(splits[0], (SEQS, LEN, D), 1.0, 6.0, ((0, 4), (1, 8)))
    query_proj = centred(splits[1], (D, KD), D ** -0.5, 0.125, ((0, 32),))
    key_proj = centred(splits[2], (D, KD), D ** -0.5, 0.125, ((0, 32),))
    value_proj = centred(splits[3], (D, D), D ** -0.5, 0.125, ((0, 32),))
    swish_proj = centred(splits[4], (D, D), D ** -0.5, 0.125, ((0, 32),))
    rank_in = centred(splits[5], (D, RANK), D ** -0.5, 0.125, ((0, 32),))
    rank_out = centred(splits[6], (KD, RANK), RANK ** -0.5, 1.5, ((0, 32),))
    decay_bias = jnp.clip(0.5 + 9.5 * jax.random.uniform(splits[7], (KD,), jnp.float32) ** shard_levels(splits[7], (KD,), ((0, 32),), -0.2, 0.2), 0.5, 10.0).astype(jnp.bfloat16)
    attn_gain = jnp.clip(1.0 + 0.1 * jax.random.normal(splits[8], (D,), jnp.float32), 0.5, 1.5).astype(jnp.bfloat16)
    head_gain = jnp.clip(1.0 + 0.1 * jax.random.normal(splits[9], (HD,), jnp.float32), 0.5, 1.5).astype(jnp.bfloat16)
    out_proj = centred(splits[10], (D, D), (D // 2) ** -0.5, 0.1875, ((0, 32),))
    mlp_gain = jnp.clip(1.0 + 0.1 * jax.random.normal(splits[11], (D,), jnp.float32), 0.5, 1.5).astype(jnp.bfloat16)
    gate_proj = centred(splits[12], (D, FF), D ** -0.5, 0.125, ((0, 32),))
    up_proj = centred(splits[13], (D, FF), D ** -0.5, 0.125, ((0, 32),))
    down_proj = centred(splits[14], (FF, D), FF ** -0.5, 0.078125, ((0, 32),))
    cotangent = centred(splits[15], (SEQS, LEN, D), 1.0, 6.0, ((0, 4), (1, 8)))
    return dict(tokens=tokens, query_proj=query_proj, key_proj=key_proj, value_proj=value_proj, swish_proj=swish_proj, rank_in=rank_in, rank_out=rank_out, decay_bias=decay_bias, attn_gain=attn_gain, head_gain=head_gain, out_proj=out_proj, mlp_gain=mlp_gain, gate_proj=gate_proj, up_proj=up_proj, down_proj=down_proj, cotangent=cotangent)


norm_eps = 1e-06
exact = lax.Precision.HIGHEST

@jax.custom_vjp
def low(v):
    return lax.optimization_barrier(v.astype(jnp.bfloat16)).astype(jnp.float32)

@jax.custom_vjp
def low_back(v):
    return v

def low_keep(v):
    return (low(v), None)

def low_pass(kept, grad):
    return (grad,)

def back_keep(v):
    return (v, None)

def back_low(kept, grad):
    return (low(grad),)
low.defvjp(low_keep, low_pass)
low_back.defvjp(back_keep, back_low)

def matmul(left, right):
    return jnp.dot(left, right, precision=exact, preferred_element_type=jnp.float32)

def norm_rows(values, gain):
    return values * lax.rsqrt(lax.optimization_barrier(jnp.mean(values * values, axis=-1, keepdims=True)) + norm_eps) * gain

def block_step(kv_state, block_data):
    queries, keys_in, values_in, log_decay = block_data
    span_len = queries.shape[-2]
    scaling = queries.shape[-1] ** (-0.5)
    cumulative = jnp.cumsum(log_decay, axis=-2)
    last_row = cumulative[..., span_len - 1:, :]
    mid_row = cumulative[..., span_len // 2:span_len // 2 + 1, :]
    query_state = queries * jnp.exp(cumulative) * scaling
    carried = jnp.einsum('shck,shkv->shcv', query_state, kv_state, precision=exact)
    query_mid = queries * jnp.exp(cumulative - mid_row) * scaling
    key_mid = keys_in * jnp.exp(mid_row - cumulative)
    scores = jnp.einsum('shik,shjk->shij', query_mid, key_mid, precision=exact)
    causal = jnp.arange(span_len)[:, None] >= jnp.arange(span_len)[None, :]
    scores = jnp.where(causal, scores, 0.0)
    within = jnp.einsum('shij,shjv->shiv', scores, values_in, precision=exact)
    key_last = keys_in * jnp.exp(last_row - cumulative)
    new_state = jnp.exp(last_row[..., 0, :])[..., None] * kv_state + jnp.einsum('shck,shcv->shkv', key_last, values_in, precision=exact)
    return (new_state, carried + within)

def to_blocks(values):
    seq_count, length, features = values.shape
    head_size = features // HEADS
    blocks = values.reshape(seq_count, length // BLOCK, BLOCK, HEADS, head_size)
    return blocks.transpose(1, 0, 3, 2, 4)

def from_blocks(blocks):
    count_blocks, seq_count, head_count, span_len, head_size = blocks.shape
    return blocks.transpose(1, 0, 3, 2, 4).reshape(seq_count, count_blocks * span_len, head_count * head_size)

def attention(queries, keys_in, values_in, log_decay):
    seq_count = queries.shape[0]
    key_size = queries.shape[-1] // HEADS
    value_size = values_in.shape[-1] // HEADS
    zero_state = jnp.zeros((seq_count, HEADS, key_size, value_size), jnp.float32)
    blocks = (to_blocks(queries), to_blocks(keys_in), to_blocks(values_in), to_blocks(log_decay))
    final_state, outputs = lax.scan(jax.checkpoint(block_step), zero_state, blocks)
    return from_blocks(outputs)

def layer(tokens, query_proj, key_proj, value_proj, swish_proj, rank_in, rank_out, decay_bias, attn_gain, head_gain, out_proj, mlp_gain, gate_proj, up_proj, down_proj):
    seq_count, length, features = tokens.shape
    normed = low(norm_rows(tokens, attn_gain))
    queries = low(low_back(matmul(normed, query_proj)))
    keys_low = low(low_back(matmul(normed, key_proj)))
    values_low = low(low_back(matmul(normed, value_proj)))
    swish_in = low_back(matmul(normed, swish_proj))
    logits = matmul(matmul(normed, rank_in), rank_out.T) + decay_bias
    log_decay = jax.nn.log_sigmoid(logits) / 16.0
    mixed = attention(queries, keys_low, values_low, log_decay)
    head_norm = norm_rows(mixed.reshape(seq_count, length, HEADS, features // HEADS), head_gain)
    gated = low(head_norm.reshape(seq_count, length, features) * jax.nn.silu(swish_in))
    hidden = tokens + low_back(matmul(gated, out_proj))
    hidden_norm = low(norm_rows(hidden, mlp_gain))
    gate_val = low_back(matmul(hidden_norm, gate_proj))
    up_val = low_back(matmul(hidden_norm, up_proj))
    product = low(jax.nn.silu(gate_val) * up_val)
    return hidden + low_back(matmul(product, down_proj))

def reference(tokens, query_proj, key_proj, value_proj, swish_proj, rank_in, rank_out, decay_bias, attn_gain, head_gain, out_proj, mlp_gain, gate_proj, up_proj, down_proj, cotangent):
    members = (tokens, query_proj, key_proj, value_proj, swish_proj, rank_in, rank_out, decay_bias, attn_gain, head_gain, out_proj, mlp_gain, gate_proj, up_proj, down_proj)
    wide = [member.astype(jnp.float32) for member in members]
    result, pullback = jax.vjp(layer, *wide)
    grads = pullback(cotangent.astype(jnp.float32))
    return (result.astype(jnp.bfloat16), grads[0].astype(jnp.bfloat16), grads[1], grads[2], grads[3], grads[4], grads[5], grads[6], grads[7], grads[8], grads[9], grads[10], grads[11], grads[12], grads[13], grads[14])
```

```python
import functools

import jax
import jax.numpy as jnp
from jax import lax
from jax.experimental import pallas as pl
from jax.experimental.pallas import tpu as pltpu
from jax.sharding import Mesh, PartitionSpec as P

HEADS = 4
BLOCK = 64
EPS = 1e-06
F32 = jnp.float32
BF16 = jnp.bfloat16
EXACT = lax.Precision.HIGHEST
WAYS = ("y", "core", "hi", "t")


def to_partner(value, r):
    return lax.ppermute(value, "t", [(s, s ^ r) for s in range(HEADS)])


def swap(value, axis):
    return lax.ppermute(value, axis, [(0, 1), (1, 0)])


def natural(pieces):
    t = lax.axis_index("t")
    odd, high = (t & 1) == 1, (t & 2) == 2
    a, b, c, d = pieces
    a, b = jnp.where(odd, b, a), jnp.where(odd, a, b)
    c, d = jnp.where(odd, d, c), jnp.where(odd, c, d)
    return (
        jnp.where(high, c, a),
        jnp.where(high, d, b),
        jnp.where(high, a, c),
        jnp.where(high, b, d),
    )


def gather_rows(value):
    return jnp.concatenate([value] + [to_partner(value, r) for r in range(1, HEADS)])


def scatter_rows(value):
    rows = value.shape[0] // HEADS
    parts = [value[r * rows : (r + 1) * rows] for r in range(HEADS)]
    total = parts[0].astype(F32)
    for r in range(1, HEADS):
        total = total + to_partner(parts[r], r).astype(F32)
    return total


def stage(value, axis):
    if lax.axis_size(axis) != 2:
        return lax.all_gather(value, axis, axis=0, tiled=True)
    other = swap(value, axis)
    first = lax.axis_index(axis) == 0
    return jnp.concatenate([jnp.where(first, value, other), jnp.where(first, other, value)])


def stage_core(value):
    other = swap(value, "core")
    first = lax.axis_index("core") == 0
    half = value.shape[0] // 2
    out = []
    for i in range(2):
        v, o = value[i * half : (i + 1) * half], other[i * half : (i + 1) * half]
        out += [jnp.where(first, v, o), jnp.where(first, o, v)]
    return jnp.concatenate(out)


def slices_for(parts):
    four = []
    for n in range(HEADS):
        cols = [p[:, n * (p.shape[1] // HEADS) : (n + 1) * (p.shape[1] // HEADS)] for p in parts]
        four.append(jnp.concatenate(cols, axis=1) if len(cols) > 1 else cols[0])
    return natural(four)


def exchange_columns(parts):
    sent = slices_for(parts)
    got = [sent[0]] + [to_partner(sent[r], r) for r in range(1, HEADS)]
    return jnp.concatenate(natural(got))


def gather_columns(parts):
    return stage_core(stage(stage(exchange_columns(parts), "hi"), "y"))


def transposed(value):
    n_hi = lax.axis_size("hi")
    pairs = [
        ((i * n_hi + h) * HEADS + t, (t * n_hi + h) * HEADS + i)
        for i in range(HEADS)
        for h in range(n_hi)
        for t in range(HEADS)
    ]
    return lax.ppermute(value, WAYS, pairs)


def dot(a, b, precision=None):
    return jnp.dot(a, b, precision=precision, preferred_element_type=F32)


def dot_nt(a, b, precision=None):
    return lax.dot_general(
        a, b, (((1,), (1,)), ((), ())), precision=precision, preferred_element_type=F32
    )


def dot_tn(a, b, precision=None):
    return lax.dot_general(
        a, b, (((0,), (0,)), ((), ())), precision=precision, preferred_element_type=F32
    )


def lower(n, kind=F32):
    return (
        lax.broadcasted_iota(jnp.int32, (n, n), 0) >= lax.broadcasted_iota(jnp.int32, (n, n), 1)
    ).astype(kind)


def upper(n, kind=F32):
    return (
        lax.broadcasted_iota(jnp.int32, (n, n), 0) <= lax.broadcasted_iota(jnp.int32, (n, n), 1)
    ).astype(kind)


def running(log_decay):
    return dot(lower(log_decay.shape[0]), log_decay, EXACT)


def state_kernel(t_ref, k_ref, v_ref, ld_ref, end_ref, total_ref, state, total):
    step = pl.program_id(0)

    @pl.when(step == 0)
    def _():
        state[...] = jnp.zeros_like(state)
        total[...] = jnp.zeros_like(total)

    cum = running(ld_ref[...])
    last = cum[BLOCK - 1 :, :]
    key_last = (k_ref[...].astype(F32) * jnp.exp(last - cum)).astype(BF16)
    state[...] = state[...] * jnp.exp(last) + dot_tn(v_ref[...], key_last)
    total[...] += last

    @pl.when(step == pl.num_programs(0) - 1)
    def _():
        end_ref[...] = state[...].astype(BF16)
        total_ref[...] = total[...]


def forward_kernel(
    t_ref, q_ref, k_ref, v_ref, ld_ref, sw_ref, gain_ref, in_ref,
    gated_ref, mixed_ref, saved_ref, state,
):
    @pl.when(pl.program_id(0) == 0)
    def _():
        state[...] = in_ref[...].astype(F32)

    cum = running(ld_ref[...])
    last, mid = cum[BLOCK - 1 :, :], cum[BLOCK // 2 : BLOCK // 2 + 1, :]
    scale = q_ref.shape[1] ** -0.5
    query = q_ref[...].astype(F32) * scale
    key = k_ref[...].astype(F32)
    value = v_ref[...]
    query_state = (query * jnp.exp(cum)).astype(BF16)
    query_mid = (query * jnp.exp(cum - mid)).astype(BF16)
    key_mid = (key * jnp.exp(mid - cum)).astype(BF16)
    key_last = (key * jnp.exp(last - cum)).astype(BF16)
    low = state[...].astype(BF16)
    saved_ref[0] = low
    scores = jnp.where(lower(BLOCK) > 0, dot_nt(query_mid, key_mid), 0.0).astype(BF16)
    mixed = dot_nt(query_state, low) + dot(scores, value)
    state[...] = state[...] * jnp.exp(last) + dot_tn(value, key_last)
    mixed_ref[...] = mixed
    swish = sw_ref[...]
    normed = mixed * lax.rsqrt(jnp.mean(mixed * mixed, axis=-1, keepdims=True) + EPS)
    gated = normed * gain_ref[...] * (swish / (1.0 + jnp.exp(-swish)))
    gated_ref[...] = gated.astype(BF16)


def gate_back_kernel(
    t_ref, bg_ref, mixed_ref, sw_ref, gain_ref, q_ref, ld_ref,
    bm_ref, bs_ref, gain_grad_ref, direct_ref, state, total,
):
    step = pl.program_id(0)

    @pl.when(step == 0)
    def _():
        state[...] = jnp.zeros_like(state)
        total[...] = jnp.zeros_like(total)
        gain_grad_ref[...] = jnp.zeros_like(gain_grad_ref)

    mixed, swish, gain, back = mixed_ref[...], sw_ref[...], gain_ref[...], bg_ref[...]
    inv = lax.rsqrt(jnp.mean(mixed * mixed, axis=-1, keepdims=True) + EPS)
    unit = mixed * inv
    sig = 1.0 / (1.0 + jnp.exp(-swish))
    dy = back * (swish * sig)
    bs_ref[...] = (back * (unit * gain) * (sig * (1.0 + swish * (1.0 - sig)))).astype(BF16)
    gain_grad_ref[...] += jnp.sum(dy * unit, axis=0, keepdims=True)
    gdy = gain * dy
    back_mixed = inv * (gdy - unit * jnp.mean(unit * gdy, axis=-1, keepdims=True))
    low = back_mixed.astype(BF16)
    bm_ref[...] = low
    cum = running(ld_ref[...])
    scale = q_ref.shape[1] ** -0.5
    query_start = (q_ref[...].astype(F32) * scale * jnp.exp(cum + total[...])).astype(BF16)
    state[...] += dot_tn(low, query_start)
    total[...] += cum[BLOCK - 1 :, :]

    @pl.when(step == pl.num_programs(0) - 1)
    def _():
        direct_ref[...] = state[...].astype(BF16)


def backward_kernel(
    t_ref, q_ref, k_ref, v_ref, ld_ref, sig_ref, bm_ref, saved_ref, out_ref,
    dq_ref, dk_ref, dv_ref, dl_ref, grad,
):
    @pl.when(pl.program_id(0) == 0)
    def _():
        grad[...] = out_ref[...].astype(F32)

    cum = running(ld_ref[...])
    last, mid = cum[BLOCK - 1 :, :], cum[BLOCK // 2 : BLOCK // 2 + 1, :]
    scale = q_ref.shape[1] ** -0.5
    query = q_ref[...].astype(F32)
    key = k_ref[...].astype(F32)
    value, back = v_ref[...], bm_ref[...]
    e_state = jnp.exp(cum) * scale
    e_query = jnp.exp(cum - mid) * scale
    e_key = jnp.exp(mid - cum)
    e_last = jnp.exp(last - cum)
    query_state = (query * e_state).astype(BF16)
    query_mid = (query * e_query).astype(BF16)
    key_mid = (key * e_key).astype(BF16)
    key_last = (key * e_last).astype(BF16)
    mask = lower(BLOCK) > 0
    scores = jnp.where(mask, dot_nt(query_mid, key_mid), 0.0).astype(BF16)
    back_scores = jnp.where(mask, dot_nt(back, value), 0.0).astype(BF16)
    start = saved_ref[0]
    wide = grad[...]
    low = wide.astype(BF16)
    back_query = dot(back, start) * e_state + dot(back_scores, key_mid) * e_query
    key_end = dot(value, low) * e_last
    back_key = dot_tn(back_scores, query_mid) * e_key + key_end
    dv_ref[...] = (dot_tn(scores, back) + dot_nt(key_last, low)).astype(BF16)
    dq_ref[...] = back_query.astype(BF16)
    dk_ref[...] = back_key.astype(BF16)
    at_end = jnp.exp(last) * jnp.sum(start.astype(F32) * wide, axis=0, keepdims=True)
    at_end = at_end + jnp.sum(key * key_end, axis=0, keepdims=True)
    back_cum = query * back_query - key * back_key
    back_decay = dot(upper(BLOCK), back_cum, EXACT) + at_end
    dl_ref[...] = back_decay * sig_ref[...]
    grad[...] = wide * jnp.exp(last) + dot_tn(back, query_state)


def recurrence_calls(rows, local, key_size, value_size):
    blocks = rows // BLOCK
    each = local // BLOCK

    def at(step, t_ref):
        return jnp.bitwise_xor(step // each, t_ref[0]) * each + step % each

    def ahead(width):
        return pl.BlockSpec((BLOCK, width), lambda s, t_ref: (at(s, t_ref), 0))

    def behind(width):
        return pl.BlockSpec((BLOCK, width), lambda s, t_ref: (at(blocks - 1 - s, t_ref), 0))

    def whole(*shape):
        return pl.BlockSpec(shape, lambda s, t_ref: (0,) * len(shape))

    def shape(*dims, kind=BF16):
        return jax.ShapeDtypeStruct(dims, kind)

    params = pltpu.CompilerParams(
        dimension_semantics=("arbitrary",), vmem_limit_bytes=24 * 1024 * 1024
    )
    k, v = key_size, value_size

    def call(kernel, ins, outs, out_shape, scratch, flops, moved):
        return pl.pallas_call(
            kernel,
            grid_spec=pltpu.PrefetchScalarGridSpec(
                num_scalar_prefetch=1,
                grid=(blocks,),
                in_specs=ins,
                out_specs=outs,
                scratch_shapes=scratch,
            ),
            out_shape=out_shape,
            compiler_params=params,
            cost_estimate=pl.CostEstimate(
                flops=flops, transcendentals=rows * k * 4, bytes_accessed=moved
            ),
        )

    unit = 2 * rows * k * v
    state = call(
        state_kernel,
        [ahead(k), ahead(v), ahead(k)],
        [whole(v, k), whole(1, k)],
        [shape(v, k), shape(1, k, kind=F32)],
        [pltpu.VMEM((v, k), F32), pltpu.VMEM((1, k), F32)],
        unit,
        rows * (6 * k + 2 * v),
    )
    forward = call(
        forward_kernel,
        [ahead(k), ahead(k), ahead(v), ahead(k), ahead(v), whole(1, v), whole(v, k)],
        [ahead(v), ahead(v), pl.BlockSpec((1, v, k), lambda s, t_ref: (s, 0, 0))],
        [shape(rows, v), shape(rows, v, kind=F32), shape(blocks, v, k)],
        [pltpu.VMEM((v, k), F32)],
        3 * unit,
        rows * (8 * k + 12 * v),
    )
    gate_back = call(
        gate_back_kernel,
        [ahead(v), ahead(v), ahead(v), whole(1, v), ahead(k), ahead(k)],
        [ahead(v), ahead(v), whole(1, v), whole(v, k)],
        [shape(rows, v), shape(rows, v), shape(1, v, kind=F32), shape(v, k)],
        [pltpu.VMEM((v, k), F32), pltpu.VMEM((1, k), F32)],
        unit,
        rows * (6 * k + 16 * v),
    )
    backward = call(
        backward_kernel,
        [
            behind(k), behind(k), behind(v), behind(k), behind(k), behind(v),
            pl.BlockSpec((1, v, k), lambda s, t_ref: (blocks - 1 - s, 0, 0)), whole(v, k),
        ],
        [behind(k), behind(k), behind(v), behind(k)],
        [shape(rows, k), shape(rows, k), shape(rows, v), shape(rows, k, kind=F32)],
        [pltpu.VMEM((v, k), F32)],
        6 * unit,
        rows * (16 * k + 8 * v),
    )
    return state, forward, gate_back, backward


def chain(local, total, upward):
    n = lax.axis_size("hi")
    entering = jnp.zeros(local.shape, BF16)
    keep = jnp.exp(total)
    for s in range(n - 1):
        leaving = local
        if s:
            leaving = (local.astype(F32) + entering.astype(F32) * keep).astype(BF16)
        pair = (s, s + 1) if upward else (n - 1 - s, n - 2 - s)
        got = lax.ppermute(leaving, "hi", [pair])
        entering = entering + got if s else got
    return entering


def inverse(values):
    return lax.rsqrt(jnp.mean(values * values, axis=-1, keepdims=True) + EPS)


def norm_back(values, gain, dy):
    inv = inverse(values)
    unit = values * inv
    gdy = gain * dy
    dx = inv * (gdy - unit * jnp.mean(unit * gdy, axis=-1, keepdims=True))
    return dx, jnp.sum(dy * unit, axis=0)


def per_device(
    tokens,
    query_proj,
    key_proj,
    value_proj,
    swish_proj,
    rank_in,
    rank_out,
    decay_bias,
    attn_gain,
    head_gain,
    out_proj,
    mlp_gain,
    gate_proj,
    up_proj,
    down_proj,
    cotangent,
):
    _, local, width = tokens.shape
    t = lax.axis_index("t")
    devices = 1
    for axis in WAYS:
        devices *= lax.axis_size(axis)
    rank = rank_in.shape[1]
    keys_all = query_proj.shape[1]
    key_size, value_size = keys_all // HEADS, width // HEADS
    rows = local * HEADS

    small = (
        attn_gain, mlp_gain, head_gain, decay_bias, rank_in.reshape(-1), rank_out.reshape(-1),
    )
    sizes = [s.shape[0] for s in small]
    pad = -sum(sizes) % 1024
    packed = jnp.concatenate(small + (jnp.zeros((pad,), BF16),))
    packed = lax.all_gather(packed, WAYS, axis=0)
    got, place = [], 0
    for size in sizes:
        got.append(packed[:, place : place + size].reshape(-1))
        place += size
    attn_full, mlp_full, head_full, bias_full = [g.astype(F32) for g in got[:4]]
    rankin_full = got[4].reshape(width, rank)
    rankout_own = lax.dynamic_slice_in_dim(
        got[5].reshape(keys_all, rank), t * key_size, key_size, 0
    ).astype(F32)
    bias_own = lax.dynamic_slice_in_dim(bias_full, t * key_size, key_size, 0)

    residual = tokens[0].astype(F32)
    tokens_all = gather_rows(tokens[0])
    kv_full = gather_columns((key_proj, value_proj))
    qs_full = gather_columns((query_proj, swish_proj))
    order = ("hi", "y", "core")
    out_full = lax.all_gather(transposed(out_proj), order, axis=0, tiled=True)
    across = ("y", "core", "hi")
    gate_full = lax.all_gather(exchange_columns((gate_proj,)), across, axis=0, tiled=True)
    up_full = lax.all_gather(exchange_columns((up_proj,)), across, axis=0, tiled=True)
    down_full = lax.all_gather(transposed(down_proj), order, axis=0, tiled=True)
    cot_all = gather_rows(cotangent[0])

    wide_all = tokens_all.astype(F32)
    unit_all = wide_all * inverse(wide_all)
    normed = (unit_all * attn_full).astype(BF16)
    kv = dot(normed, kv_full)
    key = kv[:, :key_size].astype(BF16)
    value = kv[:, key_size:].astype(BF16)
    low_rank = dot(normed, rankin_full)
    logits = dot_nt(low_rank, rankout_own, EXACT) + bias_own
    log_decay = jax.nn.log_sigmoid(logits) / 16.0
    decay_slope = jax.nn.sigmoid(-logits) / 16.0
    state_call, forward_call, gate_back_call, backward_call = recurrence_calls(
        rows, local, key_size, value_size
    )
    where = t.reshape(1).astype(jnp.int32)
    end_state, end_log = state_call(where, key, value, log_decay)
    in_state = chain(end_state, end_log, True)
    qs = dot(normed, qs_full)
    query = qs[:, :key_size].astype(BF16)
    swish_in = qs[:, key_size:]
    gain_row = head_full.reshape(1, value_size)
    gated, mixed, saved = forward_call(
        where, query, key, value, log_decay, swish_in, gain_row, in_state
    )
    hidden = residual + scatter_rows(dot(gated, out_full).astype(BF16))

    hidden_norm = (hidden * inverse(hidden) * mlp_full).astype(BF16)
    hidden_all = gather_rows(hidden_norm)
    gate_val = dot(hidden_all, gate_full)
    up_val = dot(hidden_all, up_full)
    sig = jax.nn.sigmoid(gate_val)
    silu = gate_val * sig
    product = (silu * up_val).astype(BF16)
    block_out = (hidden + scatter_rows(dot(product, down_full).astype(BF16))).astype(BF16)

    back_product = dot_nt(cot_all, down_full)
    back_gate = (back_product * up_val * (sig * (1.0 + gate_val * (1.0 - sig)))).astype(BF16)
    back_up = (back_product * silu).astype(BF16)
    back_hnorm = scatter_rows(
        (dot_nt(back_gate, gate_full) + dot_nt(back_up, up_full)).astype(BF16)
    )
    grad_down = dot_tn(product, cot_all).astype(BF16)
    grad_gate = dot_tn(hidden_all, back_gate).astype(BF16)
    grad_up = dot_tn(hidden_all, back_up).astype(BF16)
    back_hidden, grad_mlpgain = norm_back(hidden, mlp_full, back_hnorm)
    back_hidden = back_hidden + cotangent[0].astype(F32)

    back_attn = gather_rows(back_hidden.astype(BF16))
    back_gated = dot_nt(back_attn, out_full)
    grad_out = dot_tn(gated, back_attn).astype(BF16)
    back_mixed, back_swish, grad_headgain, direct = gate_back_call(
        where, back_gated, mixed, swish_in, gain_row, query, log_decay
    )
    out_state = chain(direct, end_log, False)
    back_query, back_key, back_value, back_logits = backward_call(
        where, query, key, value, log_decay, decay_slope, back_mixed, saved, out_state
    )
    back_qs = jnp.concatenate([back_query, back_swish], axis=1)
    back_kv = jnp.concatenate([back_key, back_value], axis=1)
    back_rank = dot(back_logits, rankout_own, EXACT)
    back_normed = (
        dot_nt(back_kv, kv_full)
        + dot_nt(back_qs, qs_full)
        + dot_nt(back_rank.astype(BF16), rankin_full)
    )
    grad_kv = dot_tn(normed, back_kv).astype(BF16)
    grad_qs = dot_tn(normed, back_qs).astype(BF16)
    grad_bias = jnp.sum(back_logits, axis=0)
    grad_rankout = dot_tn(back_logits, low_rank, EXACT)
    grad_rankin = dot_tn(normed, back_rank.astype(BF16))
    grad_attngain = jnp.sum(back_normed * unit_all, axis=0)
    back_tokens, _ = norm_back(residual, attn_full, scatter_rows(back_normed.astype(BF16)))
    grad_tokens = (back_hidden + back_tokens).astype(BF16)

    def columns_home(grad, widths):
        part = lax.psum_scatter(grad, across, scatter_dimension=0, tiled=True)
        own = part.shape[0] // HEADS
        sent = natural([part[n * own : (n + 1) * own] for n in range(HEADS)])
        back = natural([sent[0]] + [to_partner(sent[r], r) for r in range(1, HEADS)])
        outs, place = [], 0
        for w in widths:
            outs.append(
                jnp.concatenate([b[:, place : place + w] for b in back], axis=1).astype(F32)
            )
            place += w
        return outs

    def rows_home(grad):
        part = lax.psum_scatter(grad, order, scatter_dimension=0, tiled=True)
        return transposed(part).astype(F32)

    down_home = rows_home(grad_down)
    (gate_home,) = columns_home(grad_gate, [grad_gate.shape[1]])
    (up_home,) = columns_home(grad_up, [grad_up.shape[1]])
    out_home = rows_home(grad_out)
    query_home, swish_home = columns_home(grad_qs, [key_size, value_size])
    key_home, value_home = columns_home(grad_kv, [key_size, value_size])

    def own_head(grad):
        full = jnp.zeros((keys_all,) + grad.shape[1:], F32)
        return lax.dynamic_update_slice_in_dim(full, grad, t * key_size, 0)

    grads = (
        grad_attngain, grad_mlpgain, grad_headgain.reshape(-1), own_head(grad_bias),
        grad_rankin, own_head(grad_rankout),
    )
    packed = jnp.concatenate(
        [g.reshape(devices, -1) for g in grads] + [jnp.zeros((devices, pad), F32)], axis=1
    )
    mine = lax.psum_scatter(packed, WAYS, scatter_dimension=0, tiled=True)[0]
    homes, place = [], 0
    for size in sizes:
        homes.append(mine[place : place + size])
        place += size
    return (
        block_out[None],
        grad_tokens[None],
        query_home,
        key_home,
        value_home,
        swish_home,
        homes[4].reshape(rank_in.shape),
        homes[5].reshape(rank_out.shape),
        homes[3],
        homes[0],
        homes[2],
        out_home,
        homes[1],
        gate_home,
        up_home,
        down_home,
    )


def solution(mesh):
    dp, seq = mesh.shape["dp"], mesh.shape["seq"]
    fine = Mesh(mesh.devices.reshape(dp // 2, 2, seq // HEADS, HEADS), WAYS)
    rows, flat = P(WAYS, None), P(WAYS)
    acts = P(("y", "core"), ("hi", "t"), None)
    return jax.shard_map(
        per_device,
        mesh=fine,
        in_specs=(
            acts, rows, rows, rows, rows, rows, rows, flat, flat, flat, rows, flat, rows, rows,
            rows, acts,
        ),
        out_specs=(
            acts, acts, rows, rows, rows, rows, rows, rows, flat, flat, flat, rows, flat, rows,
            rows, rows,
        ),
        check_vma=False,
    )
```

```python
import functools

import jax
import jax.numpy as jnp
from jax import lax
from jax.experimental import pallas as pl
from jax.experimental.pallas import tpu as pltpu
from jax.sharding import Mesh, PartitionSpec as P

HEADS = 4
BLOCK = 64
EPS = 1e-06
F32 = jnp.float32
BF16 = jnp.bfloat16
EXACT = lax.Precision.HIGHEST
WAYS = ("y", "core", "hi", "t")


def to_partner(value, r):
    return lax.ppermute(value, "t", [(s, s ^ r) for s in range(HEADS)])


def swap(value, axis):
    return lax.ppermute(value, axis, [(0, 1), (1, 0)])


def natural(pieces, t=None):
    t = lax.axis_index("t") if t is None else t
    odd, high = (t & 1) == 1, (t & 2) == 2
    a, b, c, d = pieces
    a, b = jnp.where(odd, b, a), jnp.where(odd, a, b)
    c, d = jnp.where(odd, d, c), jnp.where(odd, c, d)
    return (
        jnp.where(high, c, a),
        jnp.where(high, d, b),
        jnp.where(high, a, c),
        jnp.where(high, b, d),
    )


def gather_rows(value):
    return jnp.concatenate([value] + [to_partner(value, r) for r in range(1, HEADS)])


def scatter_rows(value):
    rows = value.shape[0] // HEADS
    parts = [value[r * rows : (r + 1) * rows] for r in range(HEADS)]
    total = parts[0].astype(F32)
    for r in range(1, HEADS):
        total = total + to_partner(parts[r], r).astype(F32)
    return total


def after(value, *others):
    return lax.optimization_barrier((value,) + others)[0]


def both(value, axis):
    if lax.axis_size(axis) != 2:
        return lax.all_gather(value, axis, axis=0, tiled=True)
    other = swap(value, axis)
    first = lax.axis_index(axis) == 0
    return jnp.concatenate([jnp.where(first, value, other), jnp.where(first, other, value)])


def both_cores(value):
    other = swap(value, "core")
    first = lax.axis_index("core") == 0
    half = value.shape[0] // 2
    out = []
    for i in range(2):
        v, o = value[i * half : (i + 1) * half], other[i * half : (i + 1) * half]
        out += [jnp.where(first, v, o), jnp.where(first, o, v)]
    return jnp.concatenate(out)


def columns_in(weight):
    n = weight.shape[1] // HEADS
    sent = natural([weight[:, i * n : (i + 1) * n] for i in range(HEADS)])
    got = [sent[0]] + [to_partner(sent[r], r) for r in range(1, HEADS)]
    return jnp.concatenate(natural(got))


def columns_out(part):
    own = part.shape[0] // HEADS
    sent = natural([part[n * own : (n + 1) * own] for n in range(HEADS)])
    back = natural([sent[0]] + [to_partner(sent[r], r) for r in range(1, HEADS)])
    return jnp.concatenate(back, axis=1).astype(F32)


def row_pairs():
    n_hi = lax.axis_size("hi")
    group = HEADS * n_hi
    return [
        (group * t + i * n_hi + h, (i * n_hi + h) * HEADS + t)
        for i in range(HEADS)
        for h in range(n_hi)
        for t in range(HEADS)
    ]


def rows_in(weight):
    return lax.ppermute(weight, WAYS, row_pairs())


def rows_out(part):
    return lax.ppermute(part, WAYS, [(b, a) for a, b in row_pairs()]).astype(F32)


def cell():
    return lax.axis_index("y") * 2 + lax.axis_index("core")


def add(a, b):
    return (a.astype(F32) + b.astype(F32)).astype(BF16)


def half_hi(total):
    if lax.axis_size("hi") != 2:
        return lax.psum_scatter(total, "hi", scatter_dimension=0, tiled=True)
    first = lax.axis_index("hi") == 0
    n = total.shape[0] // 2
    low, high = total[:n], total[n:]
    return add(jnp.where(first, low, high), swap(jnp.where(first, high, low), "hi"))


def rows_in_cells(value):
    n = value.shape[0] // HEADS
    return natural([value[i * n : (i + 1) * n] for i in range(HEADS)], cell())


def dot(a, b, precision=None):
    return jnp.dot(a, b, precision=precision, preferred_element_type=F32)


def dot_nt(a, b, precision=None):
    return lax.dot_general(
        a, b, (((1,), (1,)), ((), ())), precision=precision, preferred_element_type=F32
    )


def dot_tn(a, b, precision=None):
    return lax.dot_general(
        a, b, (((0,), (0,)), ((), ())), precision=precision, preferred_element_type=F32
    )


def lower(n, kind=F32):
    return (
        lax.broadcasted_iota(jnp.int32, (n, n), 0) >= lax.broadcasted_iota(jnp.int32, (n, n), 1)
    ).astype(kind)


def upper(n, kind=F32):
    return (
        lax.broadcasted_iota(jnp.int32, (n, n), 0) <= lax.broadcasted_iota(jnp.int32, (n, n), 1)
    ).astype(kind)


def running(log_decay):
    return dot(lower(log_decay.shape[0]), log_decay, EXACT)


def state_kernel(t_ref, k_ref, v_ref, ld_ref, end_ref, total_ref, state, total):
    step = pl.program_id(0)

    @pl.when(step == 0)
    def _():
        state[...] = jnp.zeros_like(state)
        total[...] = jnp.zeros_like(total)

    cum = running(ld_ref[...])
    last = cum[BLOCK - 1 :, :]
    key_last = (k_ref[...].astype(F32) * jnp.exp(last - cum)).astype(BF16)
    state[...] = state[...] * jnp.exp(last) + dot_tn(v_ref[...], key_last)
    total[...] += last

    @pl.when(step == pl.num_programs(0) - 1)
    def _():
        end_ref[...] = state[...].astype(BF16)
        total_ref[...] = total[...]


def forward_kernel(
    t_ref, q_ref, k_ref, v_ref, ld_ref, sw_ref, gain_ref, in_ref,
    gated_ref, mixed_ref, saved_ref, state,
):
    @pl.when(pl.program_id(0) == 0)
    def _():
        state[...] = in_ref[...].astype(F32)

    cum = running(ld_ref[...])
    last, mid = cum[BLOCK - 1 :, :], cum[BLOCK // 2 : BLOCK // 2 + 1, :]
    scale = q_ref.shape[1] ** -0.5
    query = q_ref[...].astype(F32) * scale
    key = k_ref[...].astype(F32)
    value = v_ref[...]
    query_state = (query * jnp.exp(cum)).astype(BF16)
    query_mid = (query * jnp.exp(cum - mid)).astype(BF16)
    key_mid = (key * jnp.exp(mid - cum)).astype(BF16)
    key_last = (key * jnp.exp(last - cum)).astype(BF16)
    low = state[...].astype(BF16)
    saved_ref[0] = low
    scores = jnp.where(lower(BLOCK) > 0, dot_nt(query_mid, key_mid), 0.0).astype(BF16)
    mixed = dot_nt(query_state, low) + dot(scores, value)
    state[...] = state[...] * jnp.exp(last) + dot_tn(value, key_last)
    mixed_ref[...] = mixed
    swish = sw_ref[...]
    normed = mixed * lax.rsqrt(jnp.mean(mixed * mixed, axis=-1, keepdims=True) + EPS)
    gated = normed * gain_ref[...] * (swish / (1.0 + jnp.exp(-swish)))
    gated_ref[...] = gated.astype(BF16)


def gate_back_kernel(
    t_ref, bg_ref, mixed_ref, sw_ref, gain_ref, q_ref, ld_ref,
    bm_ref, bs_ref, gain_grad_ref, direct_ref, state, total,
):
    step = pl.program_id(0)

    @pl.when(step == 0)
    def _():
        state[...] = jnp.zeros_like(state)
        total[...] = jnp.zeros_like(total)
        gain_grad_ref[...] = jnp.zeros_like(gain_grad_ref)

    mixed, swish, gain, back = mixed_ref[...], sw_ref[...], gain_ref[...], bg_ref[...]
    inv = lax.rsqrt(jnp.mean(mixed * mixed, axis=-1, keepdims=True) + EPS)
    unit = mixed * inv
    sig = 1.0 / (1.0 + jnp.exp(-swish))
    dy = back * (swish * sig)
    bs_ref[...] = (back * (unit * gain) * (sig * (1.0 + swish * (1.0 - sig)))).astype(BF16)
    gain_grad_ref[...] += jnp.sum(dy * unit, axis=0, keepdims=True)
    gdy = gain * dy
    back_mixed = inv * (gdy - unit * jnp.mean(unit * gdy, axis=-1, keepdims=True))
    low = back_mixed.astype(BF16)
    bm_ref[...] = low
    cum = running(ld_ref[...])
    scale = q_ref.shape[1] ** -0.5
    query_start = (q_ref[...].astype(F32) * scale * jnp.exp(cum + total[...])).astype(BF16)
    state[...] += dot_tn(low, query_start)
    total[...] += cum[BLOCK - 1 :, :]

    @pl.when(step == pl.num_programs(0) - 1)
    def _():
        direct_ref[...] = state[...].astype(BF16)


def backward_kernel(
    t_ref, q_ref, k_ref, v_ref, ld_ref, sig_ref, bm_ref, saved_ref, out_ref,
    dq_ref, dk_ref, dv_ref, dl_ref, grad,
):
    @pl.when(pl.program_id(0) == 0)
    def _():
        grad[...] = out_ref[...].astype(F32)

    cum = running(ld_ref[...])
    last, mid = cum[BLOCK - 1 :, :], cum[BLOCK // 2 : BLOCK // 2 + 1, :]
    scale = q_ref.shape[1] ** -0.5
    query = q_ref[...].astype(F32)
    key = k_ref[...].astype(F32)
    value, back = v_ref[...], bm_ref[...]
    e_state = jnp.exp(cum) * scale
    e_query = jnp.exp(cum - mid) * scale
    e_key = jnp.exp(mid - cum)
    e_last = jnp.exp(last - cum)
    query_state = (query * e_state).astype(BF16)
    query_mid = (query * e_query).astype(BF16)
    key_mid = (key * e_key).astype(BF16)
    key_last = (key * e_last).astype(BF16)
    mask = lower(BLOCK) > 0
    scores = jnp.where(mask, dot_nt(query_mid, key_mid), 0.0).astype(BF16)
    back_scores = jnp.where(mask, dot_nt(back, value), 0.0).astype(BF16)
    start = saved_ref[0]
    wide = grad[...]
    low = wide.astype(BF16)
    back_query = dot(back, start) * e_state + dot(back_scores, key_mid) * e_query
    key_end = dot(value, low) * e_last
    back_key = dot_tn(back_scores, query_mid) * e_key + key_end
    dv_ref[...] = (dot_tn(scores, back) + dot_nt(key_last, low)).astype(BF16)
    dq_ref[...] = back_query.astype(BF16)
    dk_ref[...] = back_key.astype(BF16)
    at_end = jnp.exp(last) * jnp.sum(start.astype(F32) * wide, axis=0, keepdims=True)
    at_end = at_end + jnp.sum(key * key_end, axis=0, keepdims=True)
    back_cum = query * back_query - key * back_key
    back_decay = dot(upper(BLOCK), back_cum, EXACT) + at_end
    dl_ref[...] = back_decay * sig_ref[...]
    grad[...] = wide * jnp.exp(last) + dot_tn(back, query_state)


def recurrence_calls(rows, local, key_size, value_size):
    blocks = rows // BLOCK
    each = local // BLOCK

    def at(step, t_ref):
        return jnp.bitwise_xor(step // each, t_ref[0]) * each + step % each

    def ahead(width):
        return pl.BlockSpec((BLOCK, width), lambda s, t_ref: (at(s, t_ref), 0))

    def behind(width):
        return pl.BlockSpec((BLOCK, width), lambda s, t_ref: (at(blocks - 1 - s, t_ref), 0))

    def whole(*shape):
        return pl.BlockSpec(shape, lambda s, t_ref: (0,) * len(shape))

    def shape(*dims, kind=BF16):
        return jax.ShapeDtypeStruct(dims, kind)

    params = pltpu.CompilerParams(
        dimension_semantics=("arbitrary",), vmem_limit_bytes=24 * 1024 * 1024
    )
    k, v = key_size, value_size

    def call(kernel, ins, outs, out_shape, scratch, flops, moved):
        return pl.pallas_call(
            kernel,
            grid_spec=pltpu.PrefetchScalarGridSpec(
                num_scalar_prefetch=1,
                grid=(blocks,),
                in_specs=ins,
                out_specs=outs,
                scratch_shapes=scratch,
            ),
            out_shape=out_shape,
            compiler_params=params,
            cost_estimate=pl.CostEstimate(
                flops=flops, transcendentals=rows * k * 4, bytes_accessed=moved
            ),
        )

    unit = 2 * rows * k * v
    state = call(
        state_kernel,
        [ahead(k), ahead(v), ahead(k)],
        [whole(v, k), whole(1, k)],
        [shape(v, k), shape(1, k, kind=F32)],
        [pltpu.VMEM((v, k), F32), pltpu.VMEM((1, k), F32)],
        unit,
        rows * (6 * k + 2 * v),
    )
    forward = call(
        forward_kernel,
        [ahead(k), ahead(k), ahead(v), ahead(k), ahead(v), whole(1, v), whole(v, k)],
        [ahead(v), ahead(v), pl.BlockSpec((1, v, k), lambda s, t_ref: (s, 0, 0))],
        [shape(rows, v), shape(rows, v, kind=F32), shape(blocks, v, k)],
        [pltpu.VMEM((v, k), F32)],
        3 * unit,
        rows * (8 * k + 12 * v),
    )
    gate_back = call(
        gate_back_kernel,
        [ahead(v), ahead(v), ahead(v), whole(1, v), ahead(k), ahead(k)],
        [ahead(v), ahead(v), whole(1, v), whole(v, k)],
        [shape(rows, v), shape(rows, v), shape(1, v, kind=F32), shape(v, k)],
        [pltpu.VMEM((v, k), F32), pltpu.VMEM((1, k), F32)],
        unit,
        rows * (6 * k + 16 * v),
    )
    backward = call(
        backward_kernel,
        [
            behind(k), behind(k), behind(v), behind(k), behind(k), behind(v),
            pl.BlockSpec((1, v, k), lambda s, t_ref: (blocks - 1 - s, 0, 0)), whole(v, k),
        ],
        [behind(k), behind(k), behind(v), behind(k)],
        [shape(rows, k), shape(rows, k), shape(rows, v), shape(rows, k, kind=F32)],
        [pltpu.VMEM((v, k), F32)],
        6 * unit,
        rows * (16 * k + 8 * v),
    )
    return state, forward, gate_back, backward


def chain(local, total, upward):
    n = lax.axis_size("hi")
    entering = jnp.zeros(local.shape, BF16)
    keep = jnp.exp(total)
    for s in range(n - 1):
        leaving = local
        if s:
            leaving = (local.astype(F32) + entering.astype(F32) * keep).astype(BF16)
        pair = (s, s + 1) if upward else (n - 1 - s, n - 2 - s)
        got = lax.ppermute(leaving, "hi", [pair])
        entering = entering + got if s else got
    return entering


def inverse(values):
    return lax.rsqrt(jnp.mean(values * values, axis=-1, keepdims=True) + EPS)


def norm_back(values, gain, dy):
    inv = inverse(values)
    unit = values * inv
    gdy = gain * dy
    dx = inv * (gdy - unit * jnp.mean(unit * gdy, axis=-1, keepdims=True))
    return dx, jnp.sum(dy * unit, axis=0)


def per_device(
    tokens,
    query_proj,
    key_proj,
    value_proj,
    swish_proj,
    rank_in,
    rank_out,
    decay_bias,
    attn_gain,
    head_gain,
    out_proj,
    mlp_gain,
    gate_proj,
    up_proj,
    down_proj,
    cotangent,
):
    _, local, width = tokens.shape
    t = lax.axis_index("t")
    devices = 1
    for axis in WAYS:
        devices *= lax.axis_size(axis)
    rank = rank_in.shape[1]
    keys_all = query_proj.shape[1]
    key_size, value_size = keys_all // HEADS, width // HEADS
    rows = local * HEADS

    small = (
        attn_gain, mlp_gain, head_gain, decay_bias, rank_in.reshape(-1), rank_out.reshape(-1),
    )
    sizes = [s.shape[0] for s in small]
    pad = -sum(sizes) % 1024
    packed = jnp.concatenate(small + (jnp.zeros((pad,), BF16),))
    packed = packed.reshape(1, 8, -1)
    packed = jnp.concatenate(natural([packed] + [to_partner(packed, r) for r in range(1, HEADS)]))
    packed = both_cores(both(both(packed, "hi"), "y")).reshape(devices, -1)
    got, place = [], 0
    for size in sizes:
        got.append(packed[:, place : place + size].reshape(-1))
        place += size
    attn_full, mlp_full, head_full, bias_full = [g.astype(F32) for g in got[:4]]
    rankin_full = got[4].reshape(width, rank)
    rankout_own = lax.dynamic_slice_in_dim(
        got[5].reshape(keys_all, rank), t * key_size, key_size, 0
    ).astype(F32)
    bias_own = lax.dynamic_slice_in_dim(bias_full, t * key_size, key_size, 0)

    residual = tokens[0].astype(F32)
    key_in, value_in = columns_in(key_proj), columns_in(value_proj)
    tokens_all = gather_rows(tokens[0])
    query_in = columns_in(after(query_proj, key_in))
    swish_in_ = columns_in(after(swish_proj, value_in))
    out_in = rows_in(after(out_proj, query_in))
    gate_in = columns_in(after(gate_proj, tokens_all, swish_in_))
    up_in = columns_in(after(up_proj, gate_in))
    down_in = rows_in(after(down_proj, up_in))
    cot_all = gather_rows(after(cotangent[0], down_in))
    key_hi, value_hi = both(key_in, "hi"), both(value_in, "hi")
    query_hi = both(after(query_in, key_hi), "hi")
    swish_hi = both(after(swish_in_, value_hi), "hi")
    out_hi = both(after(out_in, query_hi), "hi")
    gate_hi = both(after(gate_in, swish_hi), "hi")
    key_full = both_cores(both(key_hi, "y"))
    value_full = both_cores(both(value_hi, "y"))
    query_full = both_cores(both(query_hi, "y"))
    swish_full = both_cores(both(swish_hi, "y"))
    out_full = both_cores(both(out_hi, "y"))
    gate_full = both_cores(both(gate_hi, "y"))

    wide_all = tokens_all.astype(F32)
    unit_all = wide_all * inverse(wide_all)
    normed = (unit_all * attn_full).astype(BF16)
    key = dot(normed, key_full).astype(BF16)
    value = dot(normed, value_full).astype(BF16)
    low_rank = dot(normed, rankin_full)
    logits = dot_nt(low_rank, rankout_own, EXACT) + bias_own
    log_decay = jax.nn.log_sigmoid(logits) / 16.0
    decay_slope = jax.nn.sigmoid(-logits) / 16.0
    state_call, forward_call, gate_back_call, backward_call = recurrence_calls(
        rows, local, key_size, value_size
    )
    where = t.reshape(1).astype(jnp.int32)
    end_state, end_log = state_call(where, key, value, log_decay)
    in_state = chain(end_state, end_log, True)
    up_hi = both(after(up_in, in_state), "hi")
    down_hi = both(after(down_in, gate_hi), "hi")
    up_full = both_cores(both(up_hi, "y"))
    down_full = both_cores(both(down_hi, "y"))
    query = dot(normed, query_full).astype(BF16)
    swish_in = dot(normed, swish_full)
    gain_row = head_full.reshape(1, value_size)
    gated, mixed, saved = forward_call(
        where, query, key, value, log_decay, swish_in, gain_row, in_state
    )
    hidden = residual + scatter_rows(dot(gated, out_full).astype(BF16))

    hidden_norm = (hidden * inverse(hidden) * mlp_full).astype(BF16)
    hidden_all = gather_rows(hidden_norm)
    gate_val = dot(hidden_all, gate_full)
    up_val = dot(hidden_all, up_full)
    sig = jax.nn.sigmoid(gate_val)
    silu = gate_val * sig
    product = (silu * up_val).astype(BF16)

    back_product = dot_nt(cot_all, down_full)
    back_gate = (back_product * up_val * (sig * (1.0 + gate_val * (1.0 - sig)))).astype(BF16)
    back_up = (back_product * silu).astype(BF16)
    back_hnorm = (dot_nt(back_gate, gate_full) + dot_nt(back_up, up_full)).astype(BF16)

    def by_columns(left, right):
        sent = [swap(dot_tn(left[r], right).astype(BF16), "core") for r in (1, 3)]
        return [
            (dot_tn(left[r], right) + got.astype(F32)).astype(BF16)
            for r, got in zip((0, 2), sent)
        ]

    def by_rows(left, right):
        cells = rows_in_cells(dot_tn(left, right).astype(BF16))
        return [add(cells[r], swap(cells[r + 1], "core")) for r in (0, 2)]

    def over_y(pair):
        return add(pair[0], swap(pair[1], "y"))

    def cells_of(value):
        n = value.shape[1] // HEADS
        return natural([value[:, i * n : (i + 1) * n] for i in range(HEADS)], cell())

    hidden_cells, normed_cells = cells_of(hidden_all), cells_of(normed)
    back_hnorm_sum = scatter_rows(back_hnorm)
    up_pair = by_columns(hidden_cells, back_up)
    gate_pair = by_columns(hidden_cells, back_gate)
    down_pair = by_rows(product, cot_all)
    back_hnorm_sum = after(back_hnorm_sum, *up_pair, *gate_pair, *down_pair)
    back_hidden, grad_mlpgain = norm_back(hidden, mlp_full, back_hnorm_sum)
    back_hidden = back_hidden + cotangent[0].astype(F32)

    back_attn = gather_rows(back_hidden.astype(BF16))
    up_y = over_y(up_pair)
    back_attn = after(back_attn, up_y)
    back_gated = dot_nt(back_attn, out_full)
    out_pair = by_rows(gated, back_attn)
    back_mixed, back_swish, grad_headgain, direct = gate_back_call(
        where, back_gated, mixed, swish_in, gain_row, query, log_decay
    )
    out_state = chain(direct, end_log, False)
    block_out = scatter_rows(dot(product, after(down_full, direct)).astype(BF16))
    block_out = (hidden + block_out).astype(BF16)
    swish_pair = by_columns(normed_cells, back_swish)
    back_query, back_key, back_value, back_logits = backward_call(
        where, query, key, value, log_decay, decay_slope, back_mixed, saved, out_state
    )
    gate_y, down_y = over_y(gate_pair), over_y(down_pair)
    back_rank = dot(back_logits, rankout_own, EXACT)
    back_normed = (
        dot_nt(back_key, key_full)
        + dot_nt(back_value, value_full)
        + dot_nt(back_query, query_full)
        + dot_nt(back_swish, swish_full)
        + dot_nt(back_rank.astype(BF16), rankin_full)
    )
    back_tokens = scatter_rows(back_normed.astype(BF16))
    value_pair = by_columns(normed_cells, back_value)
    key_pair = by_columns(normed_cells, back_key)
    query_pair = by_columns(normed_cells, back_query)
    grad_bias = jnp.sum(back_logits, axis=0)
    grad_rankout = dot_tn(back_logits, low_rank, EXACT)
    grad_rankin = dot_tn(normed, back_rank.astype(BF16))
    grad_attngain = jnp.sum(back_normed * unit_all, axis=0)
    back_tokens, _ = norm_back(residual, attn_full, back_tokens)
    grad_tokens = (back_hidden + back_tokens).astype(BF16)

    up_home = columns_out(half_hi(up_y))
    gate_home = columns_out(half_hi(gate_y))
    down_home = rows_out(half_hi(down_y))
    out_home = rows_out(half_hi(over_y(out_pair)))
    swish_home = columns_out(half_hi(over_y(swish_pair)))
    value_home = columns_out(half_hi(over_y(value_pair)))
    key_home = columns_out(half_hi(over_y(key_pair)))
    query_home = columns_out(half_hi(over_y(query_pair)))

    def own_head(grad):
        full = jnp.zeros((keys_all,) + grad.shape[1:], F32)
        return lax.dynamic_update_slice_in_dim(full, grad, t * key_size, 0)

    grads = (
        grad_attngain, grad_mlpgain, grad_headgain.reshape(-1), own_head(grad_bias),
        grad_rankin, own_head(grad_rankout),
    )
    packed = jnp.concatenate(
        [g.reshape(devices, -1) for g in grads] + [jnp.zeros((devices, pad), F32)], axis=1
    )
    eighth = packed.shape[1] // 8
    cells = rows_in_cells(packed.reshape(devices, 8, eighth))
    pair = [cells[r] + swap(cells[r + 1], "core") for r in (0, 2)]
    half = pair[0] + swap(pair[1], "y")
    if lax.axis_size("hi") == 2:
        first = lax.axis_index("hi") == 0
        low, high = half[:HEADS], half[HEADS:]
        mine = jnp.where(first, low, high) + swap(jnp.where(first, high, low), "hi")
    else:
        mine = lax.psum_scatter(half, "hi", scatter_dimension=0, tiled=True)
    parts = natural([mine[n] for n in range(HEADS)])
    mine = parts[0]
    for r in range(1, HEADS):
        mine = mine + to_partner(parts[r], r)
    mine = mine.reshape(-1)
    homes, place = [], 0
    for size in sizes:
        homes.append(mine[place : place + size])
        place += size
    return (
        block_out[None],
        grad_tokens[None],
        query_home,
        key_home,
        value_home,
        swish_home,
        homes[4].reshape(rank_in.shape),
        homes[5].reshape(rank_out.shape),
        homes[3],
        homes[0],
        homes[2],
        out_home,
        homes[1],
        gate_home,
        up_home,
        down_home,
    )


def solution(mesh):
    dp, seq = mesh.shape["dp"], mesh.shape["seq"]
    fine = Mesh(mesh.devices.reshape(dp // 2, 2, seq // HEADS, HEADS), WAYS)
    rows, flat = P(WAYS, None), P(WAYS)
    acts = P(("y", "core"), ("hi", "t"), None)
    return jax.shard_map(
        per_device,
        mesh=fine,
        in_specs=(
            acts, rows, rows, rows, rows, rows, rows, flat, flat, flat, rows, flat, rows, rows,
            rows, acts,
        ),
        out_specs=(
            acts, acts, rows, rows, rows, rows, rows, rows, flat, flat, flat, rows, flat, rows,
            rows, rows,
        ),
        check_vma=False,
    )
```

```python
import functools

import jax
import jax.numpy as jnp
from jax import lax
from jax.experimental import pallas as pl
from jax.experimental.pallas import tpu as pltpu
from jax.sharding import Mesh, PartitionSpec as P

HEADS = 4
BLOCK = 64
EPS = 1e-06
F32 = jnp.float32
BF16 = jnp.bfloat16
EXACT = lax.Precision.HIGHEST
WAYS = ("y", "core", "hi", "t")


def after(value, *others):
    return lax.optimization_barrier((value,) + others)[0]


def all_after(values, *others):
    return lax.optimization_barrier(tuple(values) + others)[: len(values)]


def swap(value, axis):
    return lax.ppermute(value, axis, [(0, 1), (1, 0)])


def partners(values):
    return tuple(
        lax.ppermute(v, "t", [(s, s ^ (r + 1)) for s in range(HEADS)])
        for r, v in enumerate(values)
    )


def natural(pieces, t=None):
    t = lax.axis_index("t") if t is None else t
    odd, high = (t & 1) == 1, (t & 2) == 2
    a, b, c, d = pieces
    a, b = jnp.where(odd, b, a), jnp.where(odd, a, b)
    c, d = jnp.where(odd, d, c), jnp.where(odd, c, d)
    return (
        jnp.where(high, c, a),
        jnp.where(high, d, b),
        jnp.where(high, a, c),
        jnp.where(high, b, d),
    )


def gather_rows(value):
    return jnp.concatenate((value,) + partners((value,) * 3))


def scatter_rows(value):
    rows = value.shape[0] // HEADS
    parts = [value[r * rows : (r + 1) * rows] for r in range(HEADS)]
    total = parts[0].astype(F32)
    for got in partners(parts[1:]):
        total = total + got.astype(F32)
    return total


def both(value, axis):
    if lax.axis_size(axis) != 2:
        return lax.all_gather(value, axis, axis=0, tiled=True)
    other = swap(value, axis)
    first = lax.axis_index(axis) == 0
    return jnp.concatenate([jnp.where(first, value, other), jnp.where(first, other, value)])


def both_cores(value):
    other = swap(value, "core")
    first = lax.axis_index("core") == 0
    half = value.shape[0] // 2
    out = []
    for i in range(2):
        v, o = value[i * half : (i + 1) * half], other[i * half : (i + 1) * half]
        out += [jnp.where(first, v, o), jnp.where(first, o, v)]
    return jnp.concatenate(out)


def columns_of(weights):
    four = []
    for i in range(HEADS):
        cols = []
        for w in weights:
            n = w.shape[1] // HEADS
            cols.append(w[:, i * n : (i + 1) * n])
        four.append(jnp.concatenate(cols, axis=1) if len(cols) > 1 else cols[0])
    return natural(four)


def columns_in(sent, *others):
    got = partners(all_after(sent[1:], *others))
    return jnp.concatenate(natural((sent[0],) + got))


def columns_out(part, widths):
    own = part.shape[0] // HEADS
    sent = natural([part[n * own : (n + 1) * own] for n in range(HEADS)])
    back = natural((sent[0],) + partners(sent[1:]))
    outs, place = [], 0
    for w in widths:
        outs.append(jnp.concatenate([b[:, place : place + w] for b in back], axis=1).astype(F32))
        place += w
    return outs


def row_pairs():
    n_hi = lax.axis_size("hi")
    group = HEADS * n_hi
    return [
        (group * t + i * n_hi + h, (i * n_hi + h) * HEADS + t)
        for i in range(HEADS)
        for h in range(n_hi)
        for t in range(HEADS)
    ]


def rows_in(weight):
    return lax.ppermute(weight, WAYS, row_pairs())


def rows_out(part):
    return lax.ppermute(part, WAYS, [(b, a) for a, b in row_pairs()]).astype(F32)


def cell():
    return lax.axis_index("y") * 2 + lax.axis_index("core")


def add(a, b):
    return (a.astype(F32) + b.astype(F32)).astype(BF16)


def half_hi(total):
    if lax.axis_size("hi") != 2:
        return lax.psum_scatter(total, "hi", scatter_dimension=0, tiled=True)
    first = lax.axis_index("hi") == 0
    n = total.shape[0] // 2
    low, high = total[:n], total[n:]
    return add(jnp.where(first, low, high), swap(jnp.where(first, high, low), "hi"))


def over_y(pair):
    return add(pair[0], swap(pair[1], "y"))


def rows_in_cells(value):
    n = value.shape[0] // HEADS
    return natural([value[i * n : (i + 1) * n] for i in range(HEADS)], cell())


def columns_in_cells(value):
    n = value.shape[1] // HEADS
    return natural([value[:, i * n : (i + 1) * n] for i in range(HEADS)], cell())


def by_columns(left, right):
    sent = [swap(dot_tn(left[r], right).astype(BF16), "core") for r in (1, 3)]
    return tuple(
        (dot_tn(left[r], right) + got.astype(F32)).astype(BF16) for r, got in zip((0, 2), sent)
    )


def by_rows(left, right):
    cells = rows_in_cells(dot_tn(left, right).astype(BF16))
    return tuple(add(cells[r], swap(cells[r + 1], "core")) for r in (0, 2))


def dot(a, b, precision=None):
    return jnp.dot(a, b, precision=precision, preferred_element_type=F32)


def dot_nt(a, b, precision=None):
    return lax.dot_general(
        a, b, (((1,), (1,)), ((), ())), precision=precision, preferred_element_type=F32
    )


def dot_tn(a, b, precision=None):
    return lax.dot_general(
        a, b, (((0,), (0,)), ((), ())), precision=precision, preferred_element_type=F32
    )


def lower(n, kind=F32):
    return (
        lax.broadcasted_iota(jnp.int32, (n, n), 0) >= lax.broadcasted_iota(jnp.int32, (n, n), 1)
    ).astype(kind)


def upper(n, kind=F32):
    return (
        lax.broadcasted_iota(jnp.int32, (n, n), 0) <= lax.broadcasted_iota(jnp.int32, (n, n), 1)
    ).astype(kind)


def running(log_decay):
    return dot(lower(log_decay.shape[0]), log_decay, EXACT)


def state_kernel(t_ref, k_ref, v_ref, ld_ref, end_ref, total_ref, state, total):
    step = pl.program_id(0)

    @pl.when(step == 0)
    def _():
        state[...] = jnp.zeros_like(state)
        total[...] = jnp.zeros_like(total)

    cum = running(ld_ref[...])
    last = cum[BLOCK - 1 :, :]
    key_last = (k_ref[...].astype(F32) * jnp.exp(last - cum)).astype(BF16)
    state[...] = state[...] * jnp.exp(last) + dot_tn(v_ref[...], key_last)
    total[...] += last

    @pl.when(step == pl.num_programs(0) - 1)
    def _():
        end_ref[...] = state[...].astype(BF16)
        total_ref[...] = total[...]


def forward_kernel(
    t_ref, q_ref, k_ref, v_ref, ld_ref, sw_ref, gain_ref, in_ref,
    gated_ref, mixed_ref, saved_ref, state,
):
    @pl.when(pl.program_id(0) == 0)
    def _():
        state[...] = in_ref[...].astype(F32)

    cum = running(ld_ref[...])
    last, mid = cum[BLOCK - 1 :, :], cum[BLOCK // 2 : BLOCK // 2 + 1, :]
    scale = q_ref.shape[1] ** -0.5
    query = q_ref[...].astype(F32) * scale
    key = k_ref[...].astype(F32)
    value = v_ref[...]
    query_state = (query * jnp.exp(cum)).astype(BF16)
    query_mid = (query * jnp.exp(cum - mid)).astype(BF16)
    key_mid = (key * jnp.exp(mid - cum)).astype(BF16)
    key_last = (key * jnp.exp(last - cum)).astype(BF16)
    low = state[...].astype(BF16)
    saved_ref[0] = low
    scores = jnp.where(lower(BLOCK) > 0, dot_nt(query_mid, key_mid), 0.0).astype(BF16)
    mixed = dot_nt(query_state, low) + dot(scores, value)
    state[...] = state[...] * jnp.exp(last) + dot_tn(value, key_last)
    mixed_ref[...] = mixed
    swish = sw_ref[...]
    normed = mixed * lax.rsqrt(jnp.mean(mixed * mixed, axis=-1, keepdims=True) + EPS)
    gated = normed * gain_ref[...] * (swish / (1.0 + jnp.exp(-swish)))
    gated_ref[...] = gated.astype(BF16)


def gate_back_kernel(
    t_ref, bg_ref, mixed_ref, sw_ref, gain_ref, q_ref, ld_ref,
    bm_ref, bs_ref, gain_grad_ref, direct_ref, state, total,
):
    step = pl.program_id(0)

    @pl.when(step == 0)
    def _():
        state[...] = jnp.zeros_like(state)
        total[...] = jnp.zeros_like(total)
        gain_grad_ref[...] = jnp.zeros_like(gain_grad_ref)

    mixed, swish, gain, back = mixed_ref[...], sw_ref[...], gain_ref[...], bg_ref[...]
    inv = lax.rsqrt(jnp.mean(mixed * mixed, axis=-1, keepdims=True) + EPS)
    unit = mixed * inv
    sig = 1.0 / (1.0 + jnp.exp(-swish))
    dy = back * (swish * sig)
    bs_ref[...] = (back * (unit * gain) * (sig * (1.0 + swish * (1.0 - sig)))).astype(BF16)
    gain_grad_ref[...] += jnp.sum(dy * unit, axis=0, keepdims=True)
    gdy = gain * dy
    back_mixed = inv * (gdy - unit * jnp.mean(unit * gdy, axis=-1, keepdims=True))
    low = back_mixed.astype(BF16)
    bm_ref[...] = low
    cum = running(ld_ref[...])
    scale = q_ref.shape[1] ** -0.5
    query_start = (q_ref[...].astype(F32) * scale * jnp.exp(cum + total[...])).astype(BF16)
    state[...] += dot_tn(low, query_start)
    total[...] += cum[BLOCK - 1 :, :]

    @pl.when(step == pl.num_programs(0) - 1)
    def _():
        direct_ref[...] = state[...].astype(BF16)


def backward_kernel(
    t_ref, q_ref, k_ref, v_ref, ld_ref, sig_ref, bm_ref, saved_ref, out_ref,
    dq_ref, dk_ref, dv_ref, dl_ref, grad,
):
    @pl.when(pl.program_id(0) == 0)
    def _():
        grad[...] = out_ref[...].astype(F32)

    cum = running(ld_ref[...])
    last, mid = cum[BLOCK - 1 :, :], cum[BLOCK // 2 : BLOCK // 2 + 1, :]
    scale = q_ref.shape[1] ** -0.5
    query = q_ref[...].astype(F32)
    key = k_ref[...].astype(F32)
    value, back = v_ref[...], bm_ref[...]
    e_state = jnp.exp(cum) * scale
    e_query = jnp.exp(cum - mid) * scale
    e_key = jnp.exp(mid - cum)
    e_last = jnp.exp(last - cum)
    query_state = (query * e_state).astype(BF16)
    query_mid = (query * e_query).astype(BF16)
    key_mid = (key * e_key).astype(BF16)
    key_last = (key * e_last).astype(BF16)
    mask = lower(BLOCK) > 0
    scores = jnp.where(mask, dot_nt(query_mid, key_mid), 0.0).astype(BF16)
    back_scores = jnp.where(mask, dot_nt(back, value), 0.0).astype(BF16)
    start = saved_ref[0]
    wide = grad[...]
    low = wide.astype(BF16)
    back_query = dot(back, start) * e_state + dot(back_scores, key_mid) * e_query
    key_end = dot(value, low) * e_last
    back_key = dot_tn(back_scores, query_mid) * e_key + key_end
    dv_ref[...] = (dot_tn(scores, back) + dot_nt(key_last, low)).astype(BF16)
    dq_ref[...] = back_query.astype(BF16)
    dk_ref[...] = back_key.astype(BF16)
    at_end = jnp.exp(last) * jnp.sum(start.astype(F32) * wide, axis=0, keepdims=True)
    at_end = at_end + jnp.sum(key * key_end, axis=0, keepdims=True)
    back_cum = query * back_query - key * back_key
    back_decay = dot(upper(BLOCK), back_cum, EXACT) + at_end
    dl_ref[...] = back_decay * sig_ref[...]
    grad[...] = wide * jnp.exp(last) + dot_tn(back, query_state)


def recurrence_calls(rows, local, key_size, value_size):
    blocks = rows // BLOCK
    each = local // BLOCK

    def at(step, t_ref):
        return jnp.bitwise_xor(step // each, t_ref[0]) * each + step % each

    def ahead(width):
        return pl.BlockSpec((BLOCK, width), lambda s, t_ref: (at(s, t_ref), 0))

    def behind(width):
        return pl.BlockSpec((BLOCK, width), lambda s, t_ref: (at(blocks - 1 - s, t_ref), 0))

    def whole(*shape):
        return pl.BlockSpec(shape, lambda s, t_ref: (0,) * len(shape))

    def shape(*dims, kind=BF16):
        return jax.ShapeDtypeStruct(dims, kind)

    params = pltpu.CompilerParams(
        dimension_semantics=("arbitrary",), vmem_limit_bytes=24 * 1024 * 1024
    )
    k, v = key_size, value_size

    def call(kernel, ins, outs, out_shape, scratch, flops, moved):
        return pl.pallas_call(
            kernel,
            grid_spec=pltpu.PrefetchScalarGridSpec(
                num_scalar_prefetch=1,
                grid=(blocks,),
                in_specs=ins,
                out_specs=outs,
                scratch_shapes=scratch,
            ),
            out_shape=out_shape,
            compiler_params=params,
            cost_estimate=pl.CostEstimate(
                flops=flops, transcendentals=rows * k * 4, bytes_accessed=moved
            ),
        )

    unit = 2 * rows * k * v
    state = call(
        state_kernel,
        [ahead(k), ahead(v), ahead(k)],
        [whole(v, k), whole(1, k)],
        [shape(v, k), shape(1, k, kind=F32)],
        [pltpu.VMEM((v, k), F32), pltpu.VMEM((1, k), F32)],
        unit,
        rows * (6 * k + 2 * v),
    )
    forward = call(
        forward_kernel,
        [ahead(k), ahead(k), ahead(v), ahead(k), ahead(v), whole(1, v), whole(v, k)],
        [ahead(v), ahead(v), pl.BlockSpec((1, v, k), lambda s, t_ref: (s, 0, 0))],
        [shape(rows, v), shape(rows, v, kind=F32), shape(blocks, v, k)],
        [pltpu.VMEM((v, k), F32)],
        3 * unit,
        rows * (8 * k + 12 * v),
    )
    gate_back = call(
        gate_back_kernel,
        [ahead(v), ahead(v), ahead(v), whole(1, v), ahead(k), ahead(k)],
        [ahead(v), ahead(v), whole(1, v), whole(v, k)],
        [shape(rows, v), shape(rows, v), shape(1, v, kind=F32), shape(v, k)],
        [pltpu.VMEM((v, k), F32), pltpu.VMEM((1, k), F32)],
        unit,
        rows * (6 * k + 16 * v),
    )
    backward = call(
        backward_kernel,
        [
            behind(k), behind(k), behind(v), behind(k), behind(k), behind(v),
            pl.BlockSpec((1, v, k), lambda s, t_ref: (blocks - 1 - s, 0, 0)), whole(v, k),
        ],
        [behind(k), behind(k), behind(v), behind(k)],
        [shape(rows, k), shape(rows, k), shape(rows, v), shape(rows, k, kind=F32)],
        [pltpu.VMEM((v, k), F32)],
        6 * unit,
        rows * (16 * k + 8 * v),
    )
    return state, forward, gate_back, backward


def chain(local, total, upward):
    n = lax.axis_size("hi")
    entering = jnp.zeros(local.shape, BF16)
    keep = jnp.exp(total)
    for s in range(n - 1):
        leaving = local
        if s:
            leaving = (local.astype(F32) + entering.astype(F32) * keep).astype(BF16)
        pair = (s, s + 1) if upward else (n - 1 - s, n - 2 - s)
        got = lax.ppermute(leaving, "hi", [pair])
        entering = entering + got if s else got
    return entering


def inverse(values):
    return lax.rsqrt(jnp.mean(values * values, axis=-1, keepdims=True) + EPS)


def norm_back(values, gain, dy):
    inv = inverse(values)
    unit = values * inv
    gdy = gain * dy
    dx = inv * (gdy - unit * jnp.mean(unit * gdy, axis=-1, keepdims=True))
    return dx, jnp.sum(dy * unit, axis=0)


def per_device(
    tokens,
    query_proj,
    key_proj,
    value_proj,
    swish_proj,
    rank_in,
    rank_out,
    decay_bias,
    attn_gain,
    head_gain,
    out_proj,
    mlp_gain,
    gate_proj,
    up_proj,
    down_proj,
    cotangent,
):
    _, local, width = tokens.shape
    t = lax.axis_index("t")
    devices = 1
    for axis in WAYS:
        devices *= lax.axis_size(axis)
    rank = rank_in.shape[1]
    keys_all = query_proj.shape[1]
    key_size, value_size = keys_all // HEADS, width // HEADS
    rows = local * HEADS

    small = (
        attn_gain, mlp_gain, head_gain, decay_bias, rank_in.reshape(-1), rank_out.reshape(-1),
    )
    sizes = [s.shape[0] for s in small]
    pad = -sum(sizes) % 1024
    packed = jnp.concatenate(small + (jnp.zeros((pad,), BF16),))
    packed = packed.reshape(1, 8, -1)
    kv_cols = columns_of((key_proj, value_proj))
    qs_cols = columns_of((query_proj, swish_proj))
    gate_cols, up_cols = columns_of((gate_proj,)), columns_of((up_proj,))
    across = ("y", "core", "hi")

    packed = jnp.concatenate(natural((packed,) + partners((packed,) * 3)))
    kv_in = columns_in(kv_cols, packed)
    packed = both(packed, "hi")
    kv_in, packed = lax.optimization_barrier((kv_in, packed))
    kv_hi = both(kv_in, "hi")
    qs_in = columns_in(qs_cols, kv_in)
    packed = both(packed, "y")
    out_in = rows_in(after(out_proj, qs_in))
    kv_hi, qs_in, packed = lax.optimization_barrier((kv_hi, qs_in, packed))
    packed = both_cores(packed).reshape(devices, -1)
    kv_y, qs_hi = both(kv_hi, "y"), both(qs_in, "hi")
    tokens_all = gather_rows(after(tokens[0], qs_in))
    kv_y, qs_hi, tokens_all, out_in = lax.optimization_barrier((kv_y, qs_hi, tokens_all, out_in))
    kv_full = both_cores(kv_y)
    gate_in = columns_in(gate_cols, tokens_all)
    gate_full = lax.all_gather(gate_in, across, axis=0, tiled=True)
    qs_y, out_hi = both(qs_hi, "y"), both(out_in, "hi")
    up_in = columns_in(up_cols, gate_in)
    up_full = lax.all_gather(up_in, across, axis=0, tiled=True)
    down_in = rows_in(after(down_proj, up_in))
    down_full = lax.all_gather(down_in, across, axis=0, tiled=True)
    got, place = [], 0
    for size in sizes:
        got.append(packed[:, place : place + size].reshape(-1))
        place += size
    attn_full, mlp_full, head_full, bias_full = [g.astype(F32) for g in got[:4]]
    rankin_full = got[4].reshape(width, rank)
    rankout_own = lax.dynamic_slice_in_dim(
        got[5].reshape(keys_all, rank), t * key_size, key_size, 0
    ).astype(F32)
    bias_own = lax.dynamic_slice_in_dim(bias_full, t * key_size, key_size, 0)

    residual = tokens[0].astype(F32)

    wide_all = tokens_all.astype(F32)
    unit_all = wide_all * inverse(wide_all)
    normed = (unit_all * attn_full).astype(BF16)
    kv = dot(normed, kv_full)
    key = kv[:, :key_size].astype(BF16)
    value = kv[:, key_size:].astype(BF16)
    low_rank = dot(normed, rankin_full)
    logits = dot_nt(low_rank, rankout_own, EXACT) + bias_own
    log_decay = jax.nn.log_sigmoid(logits) / 16.0
    decay_slope = jax.nn.sigmoid(-logits) / 16.0
    state_call, forward_call, gate_back_call, backward_call = recurrence_calls(
        rows, local, key_size, value_size
    )
    where = t.reshape(1).astype(jnp.int32)
    end_state, end_log = state_call(where, key, value, log_decay)
    end_state, qs_y, out_hi = lax.optimization_barrier((end_state, qs_y, out_hi))
    in_state = chain(end_state, end_log, True)
    out_y = both(out_hi, "y")
    qs_full = both_cores(qs_y)
    qs = dot(normed, qs_full)
    query = qs[:, :key_size].astype(BF16)
    swish_in = qs[:, key_size:]
    in_state, out_y, query, swish_in, down_in = lax.optimization_barrier(
        (in_state, out_y, query, swish_in, down_in)
    )
    out_full = both_cores(out_y)
    gain_row = head_full.reshape(1, value_size)
    gated, mixed, saved = forward_call(
        where, query, key, value, log_decay, swish_in, gain_row, in_state
    )
    attended = scatter_rows(dot(gated, out_full).astype(BF16))
    hidden = residual + attended

    hidden_norm = (hidden * inverse(hidden) * mlp_full).astype(BF16)
    hidden_all = gather_rows(hidden_norm)
    cot_all = gather_rows(after(cotangent[0], hidden_all))
    gate_val = dot(hidden_all, gate_full)
    up_val = dot(hidden_all, up_full)
    sig = jax.nn.sigmoid(gate_val)
    silu = gate_val * sig
    product = (silu * up_val).astype(BF16)

    back_product = dot_nt(cot_all, down_full)
    back_gate = (back_product * up_val * (sig * (1.0 + gate_val * (1.0 - sig)))).astype(BF16)
    back_up = (back_product * silu).astype(BF16)
    back_hnorm = (dot_nt(back_gate, gate_full) + dot_nt(back_up, up_full)).astype(BF16)

    normed_cells = columns_in_cells(normed)
    back_hnorm_sum = scatter_rows(back_hnorm)
    grad_gate = dot_tn(hidden_all, back_gate).astype(BF16)
    gate_mine = lax.psum_scatter(grad_gate, across, scatter_dimension=0, tiled=True)
    grad_up = dot_tn(hidden_all, back_up).astype(BF16)
    up_mine = lax.psum_scatter(grad_up, across, scatter_dimension=0, tiled=True)
    down_pair = by_rows(product, cot_all)
    back_hnorm_sum, down_0, down_1, grad_gate, grad_up = lax.optimization_barrier(
        (back_hnorm_sum,) + down_pair + (grad_gate, grad_up)
    )
    back_hidden, grad_mlpgain = norm_back(hidden, mlp_full, back_hnorm_sum)
    back_hidden = back_hidden + cotangent[0].astype(F32)

    down_y = over_y((down_0, down_1))
    back_attn = gather_rows(back_hidden.astype(BF16))
    back_attn, down_y = lax.optimization_barrier((back_attn, down_y))
    back_gated = dot_nt(back_attn, out_full)
    back_mixed, back_swish, grad_headgain, direct = gate_back_call(
        where, back_gated, mixed, swish_in, gain_row, query, log_decay
    )
    out_state = chain(direct, end_log, False)
    block_out = scatter_rows(dot(product, after(down_full, direct)).astype(BF16))
    block_out = (hidden + block_out).astype(BF16)
    swish_pair = by_columns(normed_cells, back_swish)
    out_pair = by_rows(gated, back_attn)
    out_state, out_0, out_1, swish_0, swish_1, down_y = lax.optimization_barrier(
        (out_state,) + out_pair + swish_pair + (down_y,)
    )
    down_mine = half_hi(down_y)
    out_y = over_y((out_0, out_1))
    back_query, back_key, back_value, back_logits = backward_call(
        where, query, key, value, log_decay, decay_slope, back_mixed, saved, out_state
    )
    back_qkv = jnp.concatenate([back_query, back_key, back_value], axis=1)
    qkv_0, qkv_1 = by_columns(normed_cells, back_qkv)
    qkv_0, qkv_1, out_y, back_qkv, back_logits = lax.optimization_barrier(
        (qkv_0, qkv_1, out_y, back_qkv, back_logits)
    )
    qkv_y = over_y((qkv_0, qkv_1))
    back_rank = dot(back_logits, rankout_own, EXACT)
    back_query, back_kv = back_qkv[:, :key_size], back_qkv[:, key_size:]
    back_qs = jnp.concatenate([back_query, back_swish], axis=1)
    back_normed = (
        dot_nt(back_kv, kv_full)
        + dot_nt(back_qs, qs_full)
        + dot_nt(back_rank.astype(BF16), rankin_full)
    )
    back_tokens = scatter_rows(back_normed.astype(BF16))
    grad_bias = jnp.sum(back_logits, axis=0)
    grad_rankout = dot_tn(back_logits, low_rank, EXACT)
    grad_rankin = dot_tn(normed, back_rank.astype(BF16))
    grad_attngain = jnp.sum(back_normed * unit_all, axis=0)
    out_mine = half_hi(after(out_y, down_mine))
    back_tokens, qkv_y, down_mine, out_mine, grad_attngain = lax.optimization_barrier(
        (back_tokens, qkv_y, down_mine, out_mine, grad_attngain)
    )
    back_tokens, _ = norm_back(residual, attn_full, back_tokens)
    grad_tokens = (back_hidden + back_tokens).astype(BF16)

    qkv_mine = half_hi(qkv_y)
    swish_y = over_y((swish_0, after(swish_1, qkv_y)))
    (gate_home,) = columns_out(after(gate_mine, qkv_y), [gate_mine.shape[1]])
    (up_home,) = columns_out(after(up_mine, gate_home), [up_mine.shape[1]])
    swish_mine = half_hi(after(swish_y, qkv_mine))
    down_home = rows_out(after(down_mine, up_home))
    out_home = rows_out(after(out_mine, down_home))
    query_home, key_home, value_home = columns_out(
        after(qkv_mine, up_home), [key_size, key_size, value_size]
    )
    (swish_home,) = columns_out(after(swish_mine, query_home), [value_size])

    def own_head(grad):
        full = jnp.zeros((keys_all,) + grad.shape[1:], F32)
        return lax.dynamic_update_slice_in_dim(full, grad, t * key_size, 0)

    grads = (
        grad_attngain, grad_mlpgain, grad_headgain.reshape(-1), own_head(grad_bias),
        grad_rankin, own_head(grad_rankout),
    )
    packed = jnp.concatenate(
        [g.reshape(devices, -1) for g in grads] + [jnp.zeros((devices, pad), F32)], axis=1
    )
    eighth = packed.shape[1] // 8
    cells = rows_in_cells(packed.reshape(devices, 8, eighth))
    pair = [cells[r] + swap(cells[r + 1], "core") for r in (0, 2)]
    half = pair[0] + swap(pair[1], "y")
    if lax.axis_size("hi") == 2:
        first = lax.axis_index("hi") == 0
        one, two = half[:HEADS], half[HEADS:]
        mine = jnp.where(first, one, two) + swap(jnp.where(first, two, one), "hi")
    else:
        mine = lax.psum_scatter(half, "hi", scatter_dimension=0, tiled=True)
    parts = natural([mine[n] for n in range(HEADS)])
    mine = parts[0]
    for got in partners(parts[1:]):
        mine = mine + got
    mine = mine.reshape(-1)
    homes, place = [], 0
    for size in sizes:
        homes.append(mine[place : place + size])
        place += size
    return (
        block_out[None],
        grad_tokens[None],
        query_home,
        key_home,
        value_home,
        swish_home,
        homes[4].reshape(rank_in.shape),
        homes[5].reshape(rank_out.shape),
        homes[3],
        homes[0],
        homes[2],
        out_home,
        homes[1],
        gate_home,
        up_home,
        down_home,
    )


def solution(mesh):
    dp, seq = mesh.shape["dp"], mesh.shape["seq"]
    fine = Mesh(mesh.devices.reshape(dp // 2, 2, seq // HEADS, HEADS), WAYS)
    rows, flat = P(WAYS, None), P(WAYS)
    acts = P(("y", "core"), ("hi", "t"), None)
    return jax.shard_map(
        per_device,
        mesh=fine,
        in_specs=(
            acts, rows, rows, rows, rows, rows, rows, flat, flat, flat, rows, flat, rows, rows,
            rows, acts,
        ),
        out_specs=(
            acts, acts, rows, rows, rows, rows, rows, rows, flat, flat, flat, rows, flat, rows,
            rows, rows,
        ),
        check_vma=False,
    )
```

```python
import functools

import jax
import jax.numpy as jnp
from jax import lax
from jax.experimental.layout import Layout, with_layout_constraint
from jax.experimental import pallas as pl
from jax.experimental.pallas import tpu as pltpu
from jax.sharding import Mesh, PartitionSpec as P

HEADS = 4
BLOCK = 64
EPS = 1e-06
F32 = jnp.float32
BF16 = jnp.bfloat16
EXACT = lax.Precision.HIGHEST
SMALL = pl.CostEstimate(flops=1, transcendentals=0, bytes_accessed=1)
WAYS = ("y", "core", "hi", "t")


def after(value, *others):
    if not others:
        return value
    return lax.optimization_barrier((value,) + others)[0]


def meet(*values):
    return lax.optimization_barrier(values)


def all_after(values, *others):
    return lax.optimization_barrier(tuple(values) + others)[: len(values)]


def by_rows_in_memory(value):
    return with_layout_constraint(value, Layout(tuple(range(value.ndim))))


def swap(value, axis):
    return lax.ppermute(value, axis, [(0, 1), (1, 0)])


def partners(values):
    return tuple(
        lax.ppermute(v, "t", [(s, s ^ (r + 1)) for s in range(HEADS)])
        for r, v in enumerate(values)
    )


def natural(pieces, t=None):
    t = lax.axis_index("t") if t is None else t
    odd, high = (t & 1) == 1, (t & 2) == 2
    a, b, c, d = pieces
    a, b = jnp.where(odd, b, a), jnp.where(odd, a, b)
    c, d = jnp.where(odd, d, c), jnp.where(odd, c, d)
    return (
        jnp.where(high, c, a),
        jnp.where(high, d, b),
        jnp.where(high, a, c),
        jnp.where(high, b, d),
    )


def gather_rows(value, until=()):
    return jnp.concatenate((after(value, *until),) + partners((value,) * 3))


def scatter_rows(value, until=()):
    rows = value.shape[0] // HEADS
    parts = [value[r * rows : (r + 1) * rows] for r in range(HEADS)]
    total = after(parts[0], *until).astype(F32)
    for got in partners(parts[1:]):
        total = total + got.astype(F32)
    return total


def over_t(value):
    t = lax.axis_index("t")
    for bit in (1, 2):
        other = lax.ppermute(value, "t", [(n, n ^ bit) for n in range(HEADS)])
        first = (t & bit) == 0
        value = jnp.concatenate([jnp.where(first, value, other), jnp.where(first, other, value)])
    return value


def both(value, axis, until=()):
    if lax.axis_size(axis) != 2:
        return lax.all_gather(value, axis, axis=0, tiled=True)
    other = swap(value, axis)
    value = after(value, *until)
    first = lax.axis_index(axis) == 0
    return jnp.concatenate([jnp.where(first, value, other), jnp.where(first, other, value)])


def both_cores(value, until=()):
    other = swap(value, "core")
    value = after(value, *until)
    first = lax.axis_index("core") == 0
    half = value.shape[0] // 2
    out = []
    for i in range(2):
        v, o = value[i * half : (i + 1) * half], other[i * half : (i + 1) * half]
        out += [jnp.where(first, v, o), jnp.where(first, o, v)]
    return jnp.concatenate(out)


def columns_of(weights):
    four = []
    for i in range(HEADS):
        cols = []
        for w in weights:
            n = w.shape[1] // HEADS
            cols.append(w[:, i * n : (i + 1) * n])
        four.append(jnp.concatenate(cols, axis=1) if len(cols) > 1 else cols[0])
    return natural(four)


def columns_in(sent, *others, until=()):
    sent = [by_rows_in_memory(part) for part in sent]
    got = partners(all_after(sent[1:], *others))
    return jnp.concatenate(natural((after(sent[0], *until),) + got))


def columns_out(part, widths, until=()):
    own = part.shape[0] // HEADS
    sent = natural([part[n * own : (n + 1) * own] for n in range(HEADS)])
    back = natural((after(sent[0], *until),) + partners(sent[1:]))
    outs, place = [], 0
    for w in widths:
        outs.append(jnp.concatenate([b[:, place : place + w] for b in back], axis=1).astype(F32))
        place += w
    return outs


def row_pairs():
    n_hi = lax.axis_size("hi")
    group = HEADS * n_hi
    return [
        (group * t + i * n_hi + h, (i * n_hi + h) * HEADS + t)
        for i in range(HEADS)
        for h in range(n_hi)
        for t in range(HEADS)
    ]


def rows_in(weight):
    return lax.ppermute(weight, WAYS, row_pairs())


def rows_out(part):
    return lax.ppermute(part, WAYS, [(b, a) for a, b in row_pairs()]).astype(F32)


def whole_lanes(width):
    return width + -width % 128


def blocks_of(weights, width):
    n_hi = lax.axis_size("hi")
    four = []
    for t in range(HEADS):
        cols = []
        for h in range(n_hi):
            for w in weights:
                for i in range(HEADS):
                    start = ((i * n_hi + h) * HEADS + t) * width
                    cols.append(w[:, start : start + width])
                cols.append(jnp.zeros((w.shape[0], -HEADS * width % 128), w.dtype))
        four.append(jnp.concatenate(cols, axis=1))
    return natural(four)


def blocks_back(part):
    own = part.shape[0] // HEADS
    sent = natural([part[n * own : (n + 1) * own] for n in range(HEADS)])
    return natural((sent[0],) + partners(sent[1:]))


def blocks_joined(back, width, count):
    n_hi = lax.axis_size("hi")
    outs = []
    for k in range(count):
        cols = []
        for i in range(HEADS):
            for h in range(n_hi):
                for t in range(HEADS):
                    start = (h * count + k) * whole_lanes(HEADS * width) + i * width
                    cols.append(back[t][:, start : start + width])
        outs.append(jnp.concatenate(cols, axis=1).astype(F32))
    return outs


def halves_in(value, until=()):
    n_hi = lax.axis_size("hi")
    width = value.shape[1] // n_hi
    cols = [value[:, n * width : (n + 1) * width] for n in range(n_hi)]
    if n_hi != 2:
        return lax.all_to_all(jnp.stack(cols), "hi", 0, 0).reshape(-1, width)
    first = lax.axis_index("hi") == 0
    kept = jnp.where(first, cols[0], cols[1])
    got = swap(jnp.where(first, cols[1], cols[0]), "hi")
    kept = after(kept, *until)
    return jnp.concatenate([jnp.where(first, kept, got), jnp.where(first, got, kept)])


def halves_out(value):
    n_hi = lax.axis_size("hi")
    rows = value.shape[0] // n_hi
    if n_hi != 2:
        got = lax.all_to_all(value.reshape(n_hi, rows, -1), "hi", 0, 0)
        return jnp.concatenate([got[n] for n in range(n_hi)], axis=1)
    first = lax.axis_index("hi") == 0
    low, high = value[:rows], value[rows:]
    kept = jnp.where(first, low, high)
    got = swap(jnp.where(first, high, low), "hi")
    return jnp.concatenate(
        [jnp.where(first, kept, got), jnp.where(first, got, kept)], axis=1
    )


def from_other(value):
    n_hi = lax.axis_size("hi")
    if n_hi == 2:
        return swap(value, "hi")
    turns = [[(s, (s + k) % n_hi) for s in range(n_hi)] for k in range(1, n_hi)]
    return jnp.concatenate([lax.ppermute(value, "hi", turn) for turn in turns])


def to_other(value):
    n_hi = lax.axis_size("hi")
    if n_hi == 2:
        return swap(value, "hi").astype(F32)
    rows = value.shape[0] // (n_hi - 1)
    total = 0.0
    for k in range(1, n_hi):
        part = value[(k - 1) * rows : k * rows]
        back = [((s + k) % n_hi, s) for s in range(n_hi)]
        total = total + lax.ppermute(part, "hi", back).astype(F32)
    return total


def cell():
    return lax.axis_index("y") * 2 + lax.axis_index("core")


def add(a, b):
    return (a.astype(F32) + b.astype(F32)).astype(BF16)


def half_hi(total, until=()):
    if lax.axis_size("hi") != 2:
        return lax.psum_scatter(total, "hi", scatter_dimension=0, tiled=True)
    first = lax.axis_index("hi") == 0
    n = total.shape[0] // 2
    low, high = total[:n], total[n:]
    kept, sent = jnp.where(first, low, high), jnp.where(first, high, low)
    return add(after(kept, *until), swap(sent, "hi"))


def over_y(pair, until=()):
    return add(after(pair[0], *until), swap(pair[1], "y"))


def rows_in_cells(value):
    n = value.shape[0] // HEADS
    return natural([value[i * n : (i + 1) * n] for i in range(HEADS)], cell())


def columns_in_cells(value):
    n = value.shape[1] // HEADS
    return natural([value[:, i * n : (i + 1) * n] for i in range(HEADS)], cell())


def by_columns(cells, right):
    theirs = jnp.concatenate([cells[1], cells[3]], axis=1)
    mine = jnp.concatenate([cells[0], cells[2]], axis=1)
    total = gradient(mine, right, swap(gradient(theirs, right), "core"))
    half = total.shape[0] // 2
    return total[:half], total[half:]


def by_rows(left, right):
    cells = rows_in_cells(dot_tn(left, right).astype(BF16))
    got = swap(jnp.concatenate([cells[1], cells[3]]), "core")
    half = cells[0].shape[0]
    return add(cells[0], got[:half]), add(cells[2], got[half:])


def dot(a, b, precision=None):
    return jnp.dot(a, b, precision=precision, preferred_element_type=F32)


def dot_nt(a, b, precision=None):
    return lax.dot_general(
        a, b, (((1,), (1,)), ((), ())), precision=precision, preferred_element_type=F32
    )


def dot_tn(a, b, precision=None):
    return lax.dot_general(
        a, b, (((0,), (0,)), ((), ())), precision=precision, preferred_element_type=F32
    )


def lower(n, kind=F32):
    return (
        lax.broadcasted_iota(jnp.int32, (n, n), 0) >= lax.broadcasted_iota(jnp.int32, (n, n), 1)
    ).astype(kind)


def upper(n, kind=F32):
    return (
        lax.broadcasted_iota(jnp.int32, (n, n), 0) <= lax.broadcasted_iota(jnp.int32, (n, n), 1)
    ).astype(kind)


def running(log_decay):
    return dot(lower(log_decay.shape[0]), log_decay, EXACT)


def state_kernel(t_ref, k_ref, v_ref, ld_ref, end_ref, total_ref, state, total):
    step = pl.program_id(0)

    @pl.when(step == 0)
    def _():
        state[...] = jnp.zeros_like(state)
        total[...] = jnp.zeros_like(total)

    cum = running(ld_ref[...])
    last = cum[BLOCK - 1 :, :]
    key_last = (k_ref[...].astype(F32) * jnp.exp(last - cum)).astype(BF16)
    state[...] = state[...] * jnp.exp(last) + dot_tn(v_ref[...], key_last)
    total[...] += last

    @pl.when(step == pl.num_programs(0) - 1)
    def _():
        end_ref[...] = state[...].astype(BF16)
        total_ref[...] = total[...]


def forward_kernel(
    t_ref, q_ref, k_ref, v_ref, ld_ref, sw_ref, gain_ref, in_ref,
    gated_ref, mixed_ref, saved_ref, state,
):
    @pl.when(pl.program_id(0) == 0)
    def _():
        state[...] = in_ref[...].astype(F32)

    cum = running(ld_ref[...])
    last, mid = cum[BLOCK - 1 :, :], cum[BLOCK // 2 : BLOCK // 2 + 1, :]
    scale = q_ref.shape[1] ** -0.5
    query = q_ref[...].astype(F32) * scale
    key = k_ref[...].astype(F32)
    value = v_ref[...]
    query_state = (query * jnp.exp(cum)).astype(BF16)
    query_mid = (query * jnp.exp(cum - mid)).astype(BF16)
    key_mid = (key * jnp.exp(mid - cum)).astype(BF16)
    key_last = (key * jnp.exp(last - cum)).astype(BF16)
    low = state[...].astype(BF16)
    saved_ref[0] = low
    scores = jnp.where(lower(BLOCK) > 0, dot_nt(query_mid, key_mid), 0.0).astype(BF16)
    mixed = dot_nt(query_state, low) + dot(scores, value)
    state[...] = state[...] * jnp.exp(last) + dot_tn(value, key_last)
    mixed_ref[...] = mixed
    swish = sw_ref[...]
    normed = mixed * lax.rsqrt(jnp.mean(mixed * mixed, axis=-1, keepdims=True) + EPS)
    gated = normed * gain_ref[...] * (swish / (1.0 + jnp.exp(-swish)))
    gated_ref[...] = gated.astype(BF16)


def gate_back_kernel(
    t_ref, bg_ref, mixed_ref, sw_ref, gain_ref, q_ref, ld_ref,
    bm_ref, bs_ref, gain_grad_ref, direct_ref, state, total,
):
    step = pl.program_id(0)

    @pl.when(step == 0)
    def _():
        state[...] = jnp.zeros_like(state)
        total[...] = jnp.zeros_like(total)
        gain_grad_ref[...] = jnp.zeros_like(gain_grad_ref)

    mixed, swish, gain, back = mixed_ref[...], sw_ref[...], gain_ref[...], bg_ref[...]
    inv = lax.rsqrt(jnp.mean(mixed * mixed, axis=-1, keepdims=True) + EPS)
    unit = mixed * inv
    sig = 1.0 / (1.0 + jnp.exp(-swish))
    dy = back * (swish * sig)
    bs_ref[...] = (back * (unit * gain) * (sig * (1.0 + swish * (1.0 - sig)))).astype(BF16)
    gain_grad_ref[...] += jnp.sum(dy * unit, axis=0, keepdims=True)
    gdy = gain * dy
    back_mixed = inv * (gdy - unit * jnp.mean(unit * gdy, axis=-1, keepdims=True))
    low = back_mixed.astype(BF16)
    bm_ref[...] = low
    cum = running(ld_ref[...])
    scale = q_ref.shape[1] ** -0.5
    query_start = (q_ref[...].astype(F32) * scale * jnp.exp(cum + total[...])).astype(BF16)
    state[...] += dot_tn(low, query_start)
    total[...] += cum[BLOCK - 1 :, :]

    @pl.when(step == pl.num_programs(0) - 1)
    def _():
        direct_ref[...] = state[...].astype(BF16)


def backward_kernel(
    t_ref, q_ref, k_ref, v_ref, ld_ref, sig_ref, bm_ref, saved_ref, out_ref,
    dq_ref, dk_ref, dv_ref, dl_ref, grad,
):
    @pl.when(pl.program_id(0) == 0)
    def _():
        grad[...] = out_ref[...].astype(F32)

    cum = running(ld_ref[...])
    last, mid = cum[BLOCK - 1 :, :], cum[BLOCK // 2 : BLOCK // 2 + 1, :]
    scale = q_ref.shape[1] ** -0.5
    query = q_ref[...].astype(F32)
    key = k_ref[...].astype(F32)
    value, back = v_ref[...], bm_ref[...]
    e_state = jnp.exp(cum) * scale
    e_query = jnp.exp(cum - mid) * scale
    e_key = jnp.exp(mid - cum)
    e_last = jnp.exp(last - cum)
    query_state = (query * e_state).astype(BF16)
    query_mid = (query * e_query).astype(BF16)
    key_mid = (key * e_key).astype(BF16)
    key_last = (key * e_last).astype(BF16)
    mask = lower(BLOCK) > 0
    scores = jnp.where(mask, dot_nt(query_mid, key_mid), 0.0).astype(BF16)
    back_scores = jnp.where(mask, dot_nt(back, value), 0.0).astype(BF16)
    start = saved_ref[0]
    wide = grad[...]
    low = wide.astype(BF16)
    back_query = dot(back, start) * e_state + dot(back_scores, key_mid) * e_query
    key_end = dot(value, low) * e_last
    back_key = dot_tn(back_scores, query_mid) * e_key + key_end
    dv_ref[...] = (dot_tn(scores, back) + dot_nt(key_last, low)).astype(BF16)
    dq_ref[...] = back_query.astype(BF16)
    dk_ref[...] = back_key.astype(BF16)
    at_end = jnp.exp(last) * jnp.sum(start.astype(F32) * wide, axis=0, keepdims=True)
    at_end = at_end + jnp.sum(key * key_end, axis=0, keepdims=True)
    back_cum = query * back_query - key * back_key
    back_decay = dot(upper(BLOCK), back_cum, EXACT) + at_end
    dl_ref[...] = back_decay * sig_ref[...]
    grad[...] = wide * jnp.exp(last) + dot_tn(back, query_state)


def recurrence_calls(rows, local, key_size, value_size):
    blocks = rows // BLOCK
    each = local // BLOCK

    def at(step, t_ref):
        return jnp.bitwise_xor(step // each, t_ref[0]) * each + step % each

    def ahead(width):
        return pl.BlockSpec((BLOCK, width), lambda s, t_ref: (at(s, t_ref), 0))

    def behind(width):
        return pl.BlockSpec((BLOCK, width), lambda s, t_ref: (at(blocks - 1 - s, t_ref), 0))

    def whole(*shape):
        return pl.BlockSpec(shape, lambda s, t_ref: (0,) * len(shape))

    def shape(*dims, kind=BF16):
        return jax.ShapeDtypeStruct(dims, kind)

    params = pltpu.CompilerParams(
        dimension_semantics=("arbitrary",), vmem_limit_bytes=24 * 1024 * 1024
    )
    k, v = key_size, value_size

    def call(kernel, ins, outs, out_shape, scratch, flops, moved):
        return pl.pallas_call(
            kernel,
            grid_spec=pltpu.PrefetchScalarGridSpec(
                num_scalar_prefetch=1,
                grid=(blocks,),
                in_specs=ins,
                out_specs=outs,
                scratch_shapes=scratch,
            ),
            out_shape=out_shape,
            compiler_params=params,
            cost_estimate=SMALL,
        )

    unit = 2 * rows * k * v
    state = call(
        state_kernel,
        [ahead(k), ahead(v), ahead(k)],
        [whole(v, k), whole(1, k)],
        [shape(v, k), shape(1, k, kind=F32)],
        [pltpu.VMEM((v, k), F32), pltpu.VMEM((1, k), F32)],
        unit,
        rows * (6 * k + 2 * v),
    )
    forward = call(
        forward_kernel,
        [ahead(k), ahead(k), ahead(v), ahead(k), ahead(v), whole(1, v), whole(v, k)],
        [ahead(v), ahead(v), pl.BlockSpec((1, v, k), lambda s, t_ref: (s, 0, 0))],
        [shape(rows, v), shape(rows, v, kind=F32), shape(blocks, v, k)],
        [pltpu.VMEM((v, k), F32)],
        3 * unit,
        rows * (8 * k + 12 * v),
    )
    gate_back = call(
        gate_back_kernel,
        [ahead(v), ahead(v), ahead(v), whole(1, v), ahead(k), ahead(k)],
        [ahead(v), ahead(v), whole(1, v), whole(v, k)],
        [shape(rows, v), shape(rows, v), shape(1, v, kind=F32), shape(v, k)],
        [pltpu.VMEM((v, k), F32), pltpu.VMEM((1, k), F32)],
        unit,
        rows * (6 * k + 16 * v),
    )
    backward = call(
        backward_kernel,
        [
            behind(k), behind(k), behind(v), behind(k), behind(k), behind(v),
            pl.BlockSpec((1, v, k), lambda s, t_ref: (blocks - 1 - s, 0, 0)), whole(v, k),
        ],
        [behind(k), behind(k), behind(v), behind(k)],
        [shape(rows, k), shape(rows, k), shape(rows, v), shape(rows, k, kind=F32)],
        [pltpu.VMEM((v, k), F32)],
        6 * unit,
        rows * (16 * k + 8 * v),
    )
    return state, forward, gate_back, backward


def kernel_call(body, grid, ins, outs, out_shape):
    return pl.pallas_call(
        body,
        grid=grid,
        in_specs=ins,
        out_specs=outs,
        out_shape=out_shape,
        compiler_params=pltpu.CompilerParams(
            dimension_semantics=("arbitrary",), vmem_limit_bytes=50 * 1024 * 1024
        ),
        cost_estimate=SMALL,
    )


def whole_block(*shape):
    return pl.BlockSpec(shape, lambda i: (0,) * len(shape), pipeline_mode=pl.Buffered(1))


def row_block(rows, width):
    return pl.BlockSpec((rows, width), lambda i: (i, 0))


def column_block(rows, width):
    return pl.BlockSpec((rows, width), lambda i: (0, i))


def project(tokens, gain, weights, rank_in, rank_out, bias, key_size, value_size):
    rows, width = tokens.shape
    rank = rank_in.shape[1]
    tile = 128
    k, v = key_size, value_size

    def body(
        x_ref, gain_ref, w_ref, in_ref, out_ref, bias_ref,
        normed_ref, inv_ref, key_ref, value_ref, query_ref, swish_ref, low_ref, ld_ref, slope_ref,
    ):
        x = x_ref[...].astype(F32)
        inv = lax.rsqrt(jnp.mean(x * x, axis=-1, keepdims=True) + EPS)
        inv_ref[...] = inv
        normed = (x * inv * gain_ref[...]).astype(BF16)
        normed_ref[...] = normed
        key_ref[...] = dot(normed, w_ref[:, :k]).astype(BF16)
        value_ref[...] = dot(normed, w_ref[:, k : k + v]).astype(BF16)
        query_ref[...] = dot(normed, w_ref[:, k + v : 2 * k + v]).astype(BF16)
        swish_ref[...] = dot(normed, w_ref[:, 2 * k + v :])
        low = dot(normed, in_ref[...])
        low_ref[...] = low
        logits = dot_nt(low, out_ref[...], EXACT) + bias_ref[...]
        small = jnp.exp(-jnp.abs(logits))
        ld_ref[...] = (jnp.minimum(logits, 0.0) - jnp.log1p(small)) / 16.0
        slope_ref[...] = jnp.where(logits > 0, small, 1.0) / (1.0 + small) / 16.0

    def out(n, kind):
        return jax.ShapeDtypeStruct((rows, n), kind)

    widths = [(width, BF16), (1, F32), (k, BF16), (v, BF16), (k, BF16), (v, F32), (rank, F32)]
    widths += [(k, F32), (k, F32)]
    return kernel_call(
        body,
        (rows // tile,),
        [
            row_block(tile, width), whole_block(1, width), whole_block(width, 2 * (k + v)),
            whole_block(width, rank), whole_block(k, rank), whole_block(1, k),
        ],
        [row_block(tile, n) for n, _ in widths],
        [out(n, kind) for n, kind in widths],
    )(tokens, gain, weights, rank_in, rank_out, bias)


def feed(hidden, cot, weights, down):
    rows, width = hidden.shape
    lanes = down.shape[0]
    tile = 512

    def body(h_ref, c_ref, w_ref, d_ref, product_ref, back_ref, hnorm_ref, low_ref):
        values = dot(h_ref[...], w_ref[...])
        gate, up = values[:, :lanes], values[:, lanes:]
        sig = 1.0 / (1.0 + jnp.exp(-gate))
        silu = gate * sig
        product = (silu * up).astype(BF16)
        product_ref[...] = product
        back = dot_nt(c_ref[...], d_ref[...])
        back_ref[:, :lanes] = (back * up * (sig * (1.0 + gate * (1.0 - sig)))).astype(BF16)
        back_ref[:, lanes:] = (back * silu).astype(BF16)
        hnorm_ref[...] = dot_nt(back_ref[...], w_ref[...]).astype(BF16)
        low_ref[...] = dot(product, d_ref[...]).astype(BF16)

    widths = [lanes, 2 * lanes, width, width]
    return kernel_call(
        body,
        (rows // tile,),
        [
            row_block(tile, width), row_block(tile, width), whole_block(*weights.shape),
            whole_block(*down.shape),
        ],
        [row_block(tile, n) for n in widths],
        [jax.ShapeDtypeStruct((rows, n), BF16) for n in widths],
    )(hidden, cot, weights, down)


def gradient(left, right, addend=None, rows=None):
    depth, width = right.shape
    rows = left.shape[1] if rows is None else rows
    tile = 512 if rows % 512 == 0 else 256

    def body(l_ref, r_ref, *refs):
        total = dot_tn(l_ref[...], r_ref[...])
        if addend is not None:
            total = total + refs[0][...].astype(F32)
        refs[-1][...] = total.astype(BF16)

    more = [] if addend is None else [addend]
    return kernel_call(
        body,
        (pl.cdiv(rows, tile),),
        [column_block(depth, tile), whole_block(depth, width)] + [row_block(tile, width) for _ in more],
        row_block(tile, width),
        jax.ShapeDtypeStruct((rows, width), BF16),
    )(left, right, *more)


def back_to_norm(back, weights, back_rank, rank_in, tokens, inv):
    rows, depth = back.shape
    width = tokens.shape[1]
    rank = rank_in.shape[1]
    tile = 512

    def body(b_ref, w_ref, br_ref, in_ref, x_ref, inv_ref, out_ref, gain_ref):
        total = dot_nt(b_ref[...], w_ref[...]) + dot_nt(br_ref[...], in_ref[...])
        out_ref[...] = total.astype(BF16)
        unit = x_ref[...].astype(F32) * inv_ref[...]
        gain_ref[...] = jnp.sum(total * unit, axis=0, keepdims=True)

    return kernel_call(
        body,
        (width // tile,),
        [
            whole_block(rows, depth), row_block(tile, depth), whole_block(rows, rank),
            row_block(tile, rank), column_block(rows, tile), whole_block(rows, 1),
        ],
        [column_block(rows, tile), column_block(1, tile)],
        [jax.ShapeDtypeStruct((rows, width), BF16), jax.ShapeDtypeStruct((1, width), F32)],
    )(back, weights, back_rank, rank_in, tokens, inv)


def chain(local, total, upward):
    n = lax.axis_size("hi")
    entering = jnp.zeros(local.shape, BF16)
    keep = jnp.exp(total)
    for s in range(n - 1):
        leaving = local
        if s:
            leaving = (local.astype(F32) + entering.astype(F32) * keep).astype(BF16)
        pair = (s, s + 1) if upward else (n - 1 - s, n - 2 - s)
        got = lax.ppermute(leaving, "hi", [pair])
        entering = entering + got if s else got
    return entering


def inverse(values):
    return lax.rsqrt(jnp.mean(values * values, axis=-1, keepdims=True) + EPS)


def norm_back(values, gain, dy):
    inv = inverse(values)
    unit = values * inv
    gdy = gain * dy
    dx = inv * (gdy - unit * jnp.mean(unit * gdy, axis=-1, keepdims=True))
    return dx, jnp.sum(dy * unit, axis=0)


def per_device(
    tokens,
    query_proj,
    key_proj,
    value_proj,
    swish_proj,
    rank_in,
    rank_out,
    decay_bias,
    attn_gain,
    head_gain,
    out_proj,
    mlp_gain,
    gate_proj,
    up_proj,
    down_proj,
    cotangent,
):
    _, local, width = tokens.shape
    t = lax.axis_index("t")
    devices = 1
    for axis in WAYS:
        devices *= lax.axis_size(axis)
    rank = rank_in.shape[1]
    keys_all = query_proj.shape[1]
    key_size, value_size = keys_all // HEADS, width // HEADS
    rows = local * HEADS

    small = (
        attn_gain, mlp_gain, head_gain, decay_bias, rank_in.reshape(-1), rank_out.reshape(-1),
    )
    sizes = [s.shape[0] for s in small]
    pad = -sum(sizes) % 1024
    packed = jnp.concatenate(small + (jnp.zeros((pad,), BF16),))
    packed = packed.reshape(1, 8, -1)
    kvqs_cols = columns_of((key_proj, value_proj, query_proj, swish_proj))
    block = down_proj.shape[0]
    gate_up_cols = blocks_of((gate_proj, up_proj), block)
    across, pair = ("y", "core", "hi"), ("y", "core")

    kvqs_in = columns_in(kvqs_cols)
    out_in = rows_in(out_proj)
    out_in = jnp.concatenate(
        [out_in[:, n * value_size : (n + 1) * value_size] for n in range(HEADS)]
    )
    attn_in = by_rows_in_memory(jnp.concatenate([kvqs_in, out_in], axis=1))
    attn_in, packed, local_tokens = meet(attn_in, packed, tokens[0])

    attn_full = lax.all_gather(attn_in, across, axis=0, tiled=True)
    tokens_all = gather_rows(local_tokens)
    packed = both_cores(both(both(over_t(packed), "hi"), "y")).reshape(devices, -1)
    tokens_all, local_cot = meet(tokens_all, cotangent[0])
    cot_own = gather_rows(local_cot)
    attn_full, tokens_all, cot_own, packed, *gate_up_cols = meet(
        attn_full, tokens_all, cot_own, packed, *gate_up_cols
    )

    gate_up_in = columns_in(gate_up_cols)
    cot_other = from_other(after(cotangent[0], tokens_all))
    kvqs_width = kvqs_in.shape[1]
    out_full = attn_full[:, kvqs_width:].reshape(-1, HEADS, out_proj.shape[0], value_size)
    out_full = jnp.concatenate(
        [out_full[:, n].reshape(value_size, value_size) for n in range(HEADS)], axis=1
    )
    down_full = jnp.pad(
        lax.all_gather(down_proj, pair, axis=0, tiled=True),
        ((0, -HEADS * block % 128), (0, 0)),
    )
    got, place = [], 0
    for size in sizes:
        got.append(packed[:, place : place + size].reshape(-1))
        place += size
    attngain_full, mlp_full, head_full, bias_full = [g.astype(F32) for g in got[:4]]
    rankin_full = got[4].reshape(width, rank)
    rankout_own = lax.dynamic_slice_in_dim(
        got[5].reshape(keys_all, rank), t * key_size, key_size, 0
    ).astype(F32)
    bias_own = lax.dynamic_slice_in_dim(bias_full, t * key_size, key_size, 0)

    residual = tokens[0].astype(F32)

    each = HEADS * block
    lanes = whole_lanes(each)
    n_hi = lax.axis_size("hi")
    normed, inv_all, key, value, query, swish_in, low_rank, log_decay, decay_slope = project(
        tokens_all, attngain_full.reshape(1, width), attn_full, rankin_full, rankout_own,
        bias_own.reshape(1, key_size), key_size, value_size,
    )
    state_call, forward_call, gate_back_call, backward_call = recurrence_calls(
        rows, local, key_size, value_size
    )
    where = t.reshape(1).astype(jnp.int32)
    end_state, end_log = state_call(where, key, value, log_decay)
    end_state, cot_other, gate_up_in = meet(end_state, cot_other, gate_up_in)

    in_state = chain(end_state, end_log, True)
    cot_other = gather_rows(cot_other)
    in_state, cot_other, gate_up_in, out_full = meet(in_state, cot_other, gate_up_in, out_full)

    gate_up_in = halves_in(gate_up_in)
    gain_row = head_full.reshape(1, value_size)
    gated, mixed, saved = forward_call(
        where, query, key, value, log_decay, swish_in, gain_row, in_state
    )
    attended = scatter_rows(dot(gated, out_full).astype(BF16))
    attended, gate_up_in = meet(attended, gate_up_in)
    gate_up_full = lax.all_gather(gate_up_in, pair, axis=0, tiled=True)

    hidden = residual + attended
    hidden_norm = (hidden * inverse(hidden) * mlp_full).astype(BF16)
    hidden_other, hidden_own = from_other(hidden_norm), gather_rows(hidden_norm)
    hidden_other = gather_rows(after(hidden_other, hidden_own))
    hidden_all = jnp.concatenate([hidden_own, hidden_other])
    cot_all = jnp.concatenate([cot_own, cot_other])
    product, back_gate_up, back_hnorm, out_low = feed(
        hidden_all, cot_all, gate_up_full, down_full
    )
    back_hnorm, back_gate_up, product, out_low = meet(back_hnorm, back_gate_up, product, out_low)

    other_sum = scatter_rows(back_hnorm[rows:]).astype(BF16)
    other_sum, back_hnorm, product = meet(other_sum, back_hnorm, product)

    own_sum, other_sum = scatter_rows(back_hnorm[:rows]), to_other(other_sum)
    own_sum, other_sum, product = meet(own_sum, other_sum, product)

    grad_down = gradient(product, cot_all, rows=each)
    normed_cells = columns_in_cells(normed)
    back_hidden, grad_mlpgain = norm_back(hidden, mlp_full, own_sum + other_sum)
    back_hidden = back_hidden + cotangent[0].astype(F32)

    back_attn = gather_rows(back_hidden.astype(BF16))
    back_attn, out_low, grad_down = meet(back_attn, out_low, grad_down)
    down_mine = lax.psum_scatter(grad_down, pair, scatter_dimension=0, tiled=True)

    back_gated = dot_nt(back_attn, out_full)
    back_mixed, back_swish, grad_headgain, direct = gate_back_call(
        where, back_gated, mixed, swish_in, gain_row, query, log_decay
    )
    out_state = chain(direct, end_log, False)
    hidden_all, direct = meet(hidden_all, direct)
    grad_gate_up = gradient(hidden_all, back_gate_up)
    gate_up_mine = lax.psum_scatter(grad_gate_up, pair, scatter_dimension=0, tiled=True)
    other_out = scatter_rows(out_low[rows:]).astype(BF16)
    out_pair = by_rows(gated, back_attn)
    out_state, out_low, other_out, out_0, out_1, grad_gate_up, down_mine = meet(
        out_state, out_low, other_out, *out_pair, grad_gate_up, down_mine
    )

    back_query, back_key, back_value, back_logits = backward_call(
        where, query, key, value, log_decay, decay_slope, back_mixed, saved, out_state
    )
    own_parts = [out_low[r * local : (r + 1) * local] for r in range(HEADS)]
    own_got = partners(own_parts[1:])
    back_kvqs = jnp.concatenate([back_key, back_value, back_query, back_swish], axis=1)
    back_kvqs, own_first = meet(back_kvqs, own_got[0])
    kvqs_pair = by_columns(normed_cells, back_kvqs)
    back_rank = dot(back_logits, rankout_own, EXACT)
    back_normed, grad_attngain = back_to_norm(
        back_kvqs, attn_full, back_rank.astype(BF16), rankin_full, tokens_all, inv_all
    )
    grad_attngain = grad_attngain[0]
    own_out = own_parts[0].astype(F32)
    for got in (own_first,) + own_got[1:]:
        own_out = own_out + got.astype(F32)
    back_low, kvqs_0, kvqs_1, other_out, own_out, gate_up_mine, out_0, out_1 = meet(
        back_normed, *kvqs_pair, other_out, own_out, gate_up_mine, out_0, out_1
    )

    back_tokens = scatter_rows(back_low)
    kvqs_y, gate_up_out = over_y((kvqs_0, kvqs_1)), halves_out(gate_up_mine)
    grad_bias = jnp.sum(back_logits, axis=0)
    grad_rankout = dot_tn(back_logits, low_rank, EXACT)
    grad_rankin = dot_tn(normed, back_rank.astype(BF16))

    def own_head(grad):
        full = jnp.zeros((keys_all,) + grad.shape[1:], F32)
        return lax.dynamic_update_slice_in_dim(full, grad, t * key_size, 0)

    grads = (
        grad_attngain, grad_mlpgain, grad_headgain.reshape(-1), own_head(grad_bias),
        grad_rankin, own_head(grad_rankout),
    )
    packed = jnp.concatenate(
        [g.reshape(devices, -1) for g in grads] + [jnp.zeros((devices, pad), F32)], axis=1
    )
    eighth = packed.shape[1] // 8
    cells = rows_in_cells(packed.reshape(devices, 8, eighth))
    back_tokens, kvqs_y, other_out, gate_up_out, out_0, out_1, *cells = meet(
        back_tokens, kvqs_y, other_out, gate_up_out, out_0, out_1, *cells
    )

    kvqs_mine, out_y = half_hi(kvqs_y), over_y((out_0, out_1))
    gate_up_back = blocks_back(gate_up_out)
    back_tokens, _ = norm_back(residual, attngain_full, back_tokens)
    grad_tokens = (back_hidden + back_tokens).astype(BF16)
    pair = [cells[r] + swap(cells[r + 1], "core") for r in (0, 2)]
    half = pair[0] + swap(pair[1], "y")
    gate_home, up_home = blocks_joined(gate_up_back, block, 2)
    kvqs_mine, out_y, other_out, half, gate_home, up_home = meet(
        kvqs_mine, out_y, other_out, half, gate_home, up_home
    )

    key_home, value_home, query_home, swish_home = columns_out(
        kvqs_mine, [key_size, value_size, key_size, value_size]
    )
    block_out = (hidden + own_out + to_other(other_out)).astype(BF16)
    out_home = rows_out(half_hi(out_y))
    down_home = down_mine.astype(F32)

    if lax.axis_size("hi") == 2:
        first = lax.axis_index("hi") == 0
        one, two = half[:HEADS], half[HEADS:]
        mine = jnp.where(first, one, two) + swap(jnp.where(first, two, one), "hi")
    else:
        mine = lax.psum_scatter(half, "hi", scatter_dimension=0, tiled=True)
    parts = natural([mine[n] for n in range(HEADS)])
    mine = parts[0]
    for got in partners(parts[1:]):
        mine = mine + got
    mine = mine.reshape(-1)
    homes, place = [], 0
    for size in sizes:
        homes.append(mine[place : place + size])
        place += size
    return (
        block_out[None],
        grad_tokens[None],
        query_home,
        key_home,
        value_home,
        swish_home,
        homes[4].reshape(rank_in.shape),
        homes[5].reshape(rank_out.shape),
        homes[3],
        homes[0],
        homes[2],
        out_home,
        homes[1],
        gate_home,
        up_home,
        down_home,
    )


def solution(mesh):
    dp, seq = mesh.shape["dp"], mesh.shape["seq"]
    fine = Mesh(mesh.devices.reshape(dp // 2, 2, seq // HEADS, HEADS), WAYS)
    rows, flat = P(WAYS, None), P(WAYS)
    acts = P(("y", "core"), ("hi", "t"), None)
    return jax.shard_map(
        per_device,
        mesh=fine,
        in_specs=(
            acts, rows, rows, rows, rows, rows, rows, flat, flat, flat, rows, flat, rows, rows,
            rows, acts,
        ),
        out_specs=(
            acts, acts, rows, rows, rows, rows, rows, rows, flat, flat, flat, rows, flat, rows,
            rows, rows,
        ),
        check_vma=False,
    )
```
